32 devices in a mesh: dp: 4 (over z), row: 2 (over x), col: 4 (over y, core).
Axes of the slice: x: 2, y: 2, z: 4, core: 2. Of those that a mesh axis runs over, the one named last changes fastest.
Arguments:
- block_input: bfloat16 [8192, 768], P(('dp', 'col'), 'row'), may hold values from -6 to 6
- w_qkv: bfloat16 [768, 2304], P('row', 'col'), may hold values from -0.21875 to 0.21875
- b_qkv: float32 [2304], P('col'), may hold values from -3 to 3
- w_in: bfloat16 [768, 3072], P('row', 'col'), may hold values from -0.21875 to 0.21875
- b_in: float32 [3072], P('col'), may hold values from -3 to 3
- w_dense: bfloat16 [768, 768], P('col', 'row'), may hold values from -1.75 to 1.75
- b_dense: float32 [768], P('row'), may hold values from -3 to 3
- w_out: bfloat16 [3072, 768], P('col', 'row'), may hold values from -0.109375 to 0.109375
- b_out: float32 [768], P('row'), may hold values from -3 to 3
- ln_attn_gain: float32 [768], P('row'), may hold values from 0.1 to 1.9
- ln_attn_bias: float32 [768], P('row'), may hold values from -2 to 2
- ln_mlp_gain: float32 [768], P('row'), may hold values from 0.1 to 1.9
- ln_mlp_bias: float32 [768], P('row'), may hold values from -2 to 2
- segments: int32 [8192], P('dp'), may hold values from 0 to 6, as said below
- positions: int32 [8192], P('dp'), may hold values from 0 to 1023, as said below
- d_out: bfloat16 [8192, 768], P(('dp', 'col'), 'row'), may hold values from -20 to 20
Outputs:
- block_output: bfloat16 [8192, 768], P(('dp', 'col'), 'row')
- d_input: float32 [8192, 768], P(('dp', 'col'), 'row')
- grad_w_qkv: float32 [768, 2304], P('row', 'col')
- grad_b_qkv: float32 [2304], P('col')
- grad_w_in: float32 [768, 3072], P('row', 'col')
- grad_b_in: float32 [3072], P('col')
- grad_w_dense: float32 [768, 768], P('col', 'row')
- grad_b_dense: float32 [768], P('row')
- grad_w_out: float32 [3072, 768], P('col', 'row')
- grad_b_out: float32 [768], P('row')
- grad_attn_gain: float32 [768], P('row')
- grad_attn_bias: float32 [768], P('row')
- grad_mlp_gain: float32 [768], P('row')
- grad_mlp_bias: float32 [768], P('row')
The draws below stay inside these ranges and needn't reach their ends.
Inputs may be any that keep to these rules, and one draw needn't show every extreme that they name: `segments`: the segment numbers of each aligned sequence of 1024 tokens start at 0 and rise by 0 or 1 from one token to the next; a document within a sequence that does not touch the sequence's ends has at least 204 tokens. `positions`: A token's position counts the tokens before it in its segment.
All inputs are finite; a program needn't handle non-finite values.
Results may differ from the reference program's by a relative error of at most 0.0093.
Values may be sent and summed in bfloat16 or wider, within the bound.
No kernel may reach another device: no remote copies, remote signals or barrier semaphores. Data moves between devices by JAX's collectives and lax.ppermute only.
A program may use at most 128 MiB of HBM per device.

```python
import math
import jax
import jax.numpy as jnp
from jax import lax

D = 768
HEADS = 12
HEAD_DIM = 64
FF = 3072
ROT = 16
SEQ_LEN = 1024
TOKENS = 8192


def packed_documents(key):
    local_key = jax.random.fold_in(key, 101)
    first_key = jax.random.fold_in(local_key, 0)
    shortest = max(SEQ_LEN // 5, 2)
    longest = 2 * SEQ_LEN
    doc_count = TOKENS // shortest + longest // shortest + 3
    random_lengths = jax.random.randint(first_key, (doc_count,), shortest, longest + 1)
    short_run = SEQ_LEN // shortest + 2
    doc_lengths = jnp.where(jnp.arange(doc_count) < short_run, shortest, random_lengths).astype(jnp.int32)
    offset_start = shortest - 1
    doc_ends = (jnp.cumsum(doc_lengths) - offset_start).astype(jnp.int32)
    token_index = jnp.arange(TOKENS, dtype=jnp.int32)
    doc_index = jnp.searchsorted(doc_ends, token_index, side='right').astype(jnp.int32)
    doc_begins = jnp.where(doc_index > 0, doc_ends[jnp.maximum(doc_index - 1, 0)], -longest).astype(jnp.int32)
    seq_begin = token_index // SEQ_LEN * SEQ_LEN
    doc_grid = doc_index.reshape(-1, SEQ_LEN)
    seg_ids = (doc_grid - doc_grid[:, :1]).reshape(-1).astype(jnp.int32)
    token_places = (token_index - jnp.maximum(doc_begins, seq_begin)).astype(jnp.int32)
    return (seg_ids, token_places)


def draw_segments(key, part):
    return packed_documents(key)[0]


def draw_positions(key, part):
    return packed_documents(key)[1]


def draw_d_out(key, part):
    first_key, second_key = jax.random.split(jax.random.fold_in(key, 202))
    ramp_place = jnp.arange(TOKENS, dtype=jnp.float32)[:, None] / max(TOKENS - 1, 1)
    base_draw = jnp.clip(jax.random.normal(first_key, (TOKENS, D), jnp.float32), -5.0, 5.0)
    ramp_scale = jnp.exp(ramp_place * math.log(3.0)) / 1.7
    rough_rows = jnp.exp(jax.random.uniform(second_key, (TOKENS, 1), jnp.float32, -0.7, 0.7))
    return (base_draw * ramp_scale * rough_rows).astype(jnp.bfloat16)


def levels(own_key, dims, cuts, smallest, top_value):
    def one(axis_at, blocks):
        heights = jax.random.uniform(jax.random.fold_in(jax.random.fold_in(own_key, 6), axis_at), (blocks,), jnp.float32, smallest / len(cuts), top_value / len(cuts))
        return jnp.repeat(jnp.exp(heights), dims[axis_at] // blocks).reshape((-1,) + (1,) * (len(dims) - axis_at - 1))

    loudness = one(*cuts[0])
    for cut in cuts[1:]:
        loudness = loudness * one(*cut)
    return loudness


def noise(own_key, shape, width, reach, cuts=(), kind=jnp.bfloat16):
    values = jax.random.normal(own_key, shape, jnp.float32) * width
    if len(cuts) > 0:
        values = levels(own_key, shape, cuts, -0.22, 0.18) * values
    return jnp.clip(values, min=-reach, max=reach).astype(kind)


def setup_inputs(seed: int = 0) -> dict:
    streams_of = jax.random.split(jax.random.key(seed), 17)
    return {
        "block_input": noise(streams_of[0], (TOKENS, D), 1.0, 6.0, ((0, 16), (1, 2))),
        "w_qkv": noise(streams_of[1], (D, 3 * D), D ** -0.5, 0.21875, ((0, 2), (1, 4))),
        "b_qkv": noise(streams_of[2], (3 * D,), 0.5, 3.0, ((0, 4),), jnp.float32),
        "w_in": noise(streams_of[3], (D, FF), D ** -0.5, 0.21875, ((0, 2), (1, 4))),
        "b_in": noise(streams_of[4], (FF,), 0.5, 3.0, ((0, 4),), jnp.float32),
        "w_dense": noise(streams_of[5], (D, D), (max(D // 64, 1)) ** -0.5, 1.75, ((0, 4), (1, 2))),
        "b_dense": noise(streams_of[6], (D,), 0.5, 3.0, ((0, 2),), jnp.float32),
        "w_out": noise(streams_of[7], (FF, D), FF ** -0.5, 0.109375, ((0, 4), (1, 2))),
        "b_out": noise(streams_of[8], (D,), 0.5, 3.0, ((0, 2),), jnp.float32),
        "ln_attn_gain": jnp.clip(1.0 + 0.18 * jax.random.normal(streams_of[9], (D,), jnp.float32), 0.1, 1.9),
        "ln_attn_bias": noise(streams_of[10], (D,), 0.3, 2.0, ((0, 2),), jnp.float32),
        "ln_mlp_gain": jnp.clip(1.0 + 0.18 * jax.random.normal(streams_of[11], (D,), jnp.float32), 0.1, 1.9),
        "ln_mlp_bias": noise(streams_of[12], (D,), 0.3, 2.0, ((0, 2),), jnp.float32),
        "segments": draw_segments(jax.random.fold_in(streams_of[16], 71), 0),
        "positions": draw_positions(jax.random.fold_in(streams_of[16], 71), 0),
        "d_out": draw_d_out(jax.random.fold_in(streams_of[16], 71), 0),
    }


@jax.custom_vjp
def low(v):
    return lax.optimization_barrier(v.astype(jnp.bfloat16)).astype(jnp.float32)

@jax.custom_vjp
def low_back(v):
    return v

def low_keep(v):
    return (low(v), None)

def low_pass(kept, grad):
    return (grad,)

def back_keep(v):
    return (v, None)

def back_low(kept, grad):
    return (low(grad),)
low.defvjp(low_keep, low_pass)
low_back.defvjp(back_keep, back_low)
EPSILON = 1e-05

def matmul_high(left_side, right_side):
    return jnp.dot(left_side, right_side, preferred_element_type=jnp.float32, precision=lax.Precision.HIGHEST)

def rotary_tables(positions):
    half_rot = ROT // 2
    freq_steps = jnp.arange(half_rot, dtype=jnp.float32) * (-2.0 * math.log(10000.0) / ROT)
    angles = positions.astype(jnp.float32)[:, None] * jnp.exp(freq_steps)[None, :]
    cos_table = jnp.concatenate([jnp.cos(angles), jnp.cos(angles)], axis=1)
    sin_table = jnp.concatenate([jnp.sin(angles), jnp.sin(angles)], axis=1)
    return (cos_table, sin_table)

def rotate_heads(joined, cos_table, sin_table):
    half_rot = ROT // 2
    cos_rows = cos_table[:, None, :]
    sin_rows = sin_table[:, None, :]

    def turned_member(member):
        leading = member[..., :ROT]
        swapped = jnp.concatenate([-leading[..., half_rot:], leading[..., :half_rot]], axis=-1)
        return jnp.concatenate([leading * cos_rows + swapped * sin_rows, member[..., ROT:]], axis=-1)
    return jnp.stack([turned_member(joined[:, :, 0]), turned_member(joined[:, :, 1]), joined[:, :, 2]], axis=2)

def attend_sequence(operands):
    query_rows, key_rows, value_rows, seg_ids = operands
    score_scale = HEAD_DIM ** (-0.5)
    scores = jnp.einsum('qhd,khd->hqk', query_rows, key_rows, precision=lax.Precision.HIGHEST) * score_scale
    scores = low_back(scores)
    places = jnp.arange(SEQ_LEN)
    allowed = (places[None, :] <= places[:, None]) & (seg_ids[None, :] == seg_ids[:, None])
    scores = jnp.where(allowed[None], scores, -jnp.inf)
    attn_probs = low(jax.nn.softmax(scores, axis=-1))
    return jnp.einsum('hqk,khd->qhd', attn_probs, value_rows, precision=lax.Precision.HIGHEST)

def layer_forward(inputs_f, w_qkv, b_qkv, w_in, b_in, w_dense, b_dense, w_out, b_out, attn_gain, attn_bias, mlp_gain, mlp_bias, segments, positions):
    mean_row = lax.optimization_barrier(jnp.mean(inputs_f, axis=1, keepdims=True))
    centered = inputs_f - mean_row
    variance = lax.optimization_barrier(jnp.mean(centered * centered, axis=1, keepdims=True))
    normed = centered * lax.rsqrt(variance + EPSILON)
    h_attn = low(normed * attn_gain + attn_bias)
    h_mlp = low(normed * mlp_gain + mlp_bias)
    joined = low_back(matmul_high(h_attn, w_qkv) + b_qkv).reshape(TOKENS, HEADS, 3, HEAD_DIM)
    cos_table, sin_table = rotary_tables(positions)
    turned = low(rotate_heads(joined, cos_table, sin_table))
    seq_count = TOKENS // SEQ_LEN
    shaped = turned.reshape(seq_count, SEQ_LEN, HEADS, 3, HEAD_DIM)
    context = lax.map(jax.checkpoint(attend_sequence), (shaped[:, :, :, 0], shaped[:, :, :, 1], shaped[:, :, :, 2], segments.reshape(seq_count, SEQ_LEN)))
    context = low(low_back(context.reshape(TOKENS, D)))
    pre_act = low_back(matmul_high(h_mlp, w_in) + b_in)
    hidden = low(jax.nn.gelu(pre_act, approximate=False))
    attn_branch = matmul_high(context, w_dense) + b_dense
    mlp_branch = matmul_high(hidden, w_out) + b_out
    return inputs_f + attn_branch + mlp_branch

def reference(block_input, w_qkv, b_qkv, w_in, b_in, w_dense, b_dense, w_out, b_out, ln_attn_gain, ln_attn_bias, ln_mlp_gain, ln_mlp_bias, segments, positions, d_out):
    floats = [member.astype(jnp.float32) for member in (block_input, w_qkv, b_qkv, w_in, b_in, w_dense, b_dense, w_out, b_out, ln_attn_gain, ln_attn_bias, ln_mlp_gain, ln_mlp_bias)]

    def wrapped(*params):
        return layer_forward(*params, segments, positions)
    result, pullback = jax.vjp(wrapped, *floats)
    grads = pullback(d_out.astype(jnp.float32))
    return (result.astype(jnp.bfloat16), grads[0], grads[1], grads[2], grads[3], grads[4], grads[5], grads[6], grads[7], grads[8], grads[9], grads[10], grads[11], grads[12])
```

```python
import math

import jax
import jax.numpy as jnp
from jax import lax
from jax.experimental import pallas as pl
from jax.experimental.pallas import tpu as pltpu
from jax.sharding import PartitionSpec as P

D = 768
HEAD_DIM = 64
ROT = 16
SEQ_LEN = 1024
EPSILON = 1e-05
BLOCK = 256
F32 = jnp.float32
BF16 = jnp.bfloat16
GROUP = ("row", "col")


def dot_nn(a, b):
    return lax.dot_general(a, b, (((1,), (0,)), ((), ())), preferred_element_type=F32)


def dot_tn(a, b):
    return lax.dot_general(a, b, (((0,), (0,)), ((), ())), preferred_element_type=F32)


def dot_nt(a, b):
    return lax.dot_general(a, b, (((1,), (1,)), ((), ())), preferred_element_type=F32)


def normalize(x_rows):
    x = x_rows.astype(F32)
    mean = jnp.mean(x, axis=1, keepdims=True)
    centered = x - mean
    var = jnp.mean(centered * centered, axis=1, keepdims=True)
    inv_std = lax.rsqrt(var + EPSILON)
    return centered * inv_std, inv_std


def norm_back(grad, normed, inv_std):
    mean_grad = jnp.mean(grad, axis=1, keepdims=True)
    mean_cross = jnp.mean(grad * normed, axis=1, keepdims=True)
    return inv_std * (grad - mean_grad - normed * mean_cross)


def mlp_kernel(
    x_ref, go_ref, wi_o, wi_p, wo_o, wo_p, b_ref, gain_ref, bias_ref,
    mix_ref, dx_ref, gwi_o, gwi_p, gwo_o, gwo_p, vec_ref,
    acc_ip, acc_op,
):
    step = pl.program_id(0)
    half = wi_o.shape[0]

    @pl.when(step == 0)
    def _():
        gwi_o[...] = jnp.zeros_like(gwi_o)
        gwo_o[...] = jnp.zeros_like(gwo_o)
        acc_ip[...] = jnp.zeros_like(acc_ip)
        acc_op[...] = jnp.zeros_like(acc_op)
        vec_ref[...] = jnp.zeros_like(vec_ref)

    normed, inv_std = normalize(x_ref[...])
    h = (normed * gain_ref[...] + bias_ref[...]).astype(BF16)
    go = go_ref[...]
    pre = dot_nn(h[:, :half], wi_o[...]) + dot_nn(h[:, half:], wi_p[...]) + b_ref[...]
    cdf = 0.5 * (1.0 + lax.erf(pre * (2.0 ** -0.5)))
    hidden = (pre * cdf).astype(BF16)
    slope = cdf + pre * (jnp.exp(-0.5 * pre * pre) * (1.0 / math.sqrt(2.0 * math.pi)))
    mix_ref[:, :half] = dot_nn(hidden, wo_o[...])
    mix_ref[:, half:] = dot_nn(hidden, wo_p[...])
    grad_hidden = dot_nt(go[:, :half], wo_o[...]) + dot_nt(go[:, half:], wo_p[...])
    grad_pre_f = grad_hidden * slope
    grad_pre = grad_pre_f.astype(BF16)
    gwi_o[...] += dot_tn(h[:, :half], grad_pre)
    acc_ip[...] += dot_tn(h[:, half:], grad_pre)
    gwo_o[...] += dot_tn(hidden, go[:, :half])
    acc_op[...] += dot_tn(hidden, go[:, half:])
    grad_h = jnp.concatenate([dot_nt(grad_pre, wi_o[...]), dot_nt(grad_pre, wi_p[...])], axis=1)
    vec_ref[0:1, :] += jnp.sum(grad_h * normed, axis=0, keepdims=True)
    vec_ref[1:2, :] += jnp.sum(grad_h, axis=0, keepdims=True)
    vec_ref[2:3, :] += jnp.sum(grad_pre.astype(F32), axis=0, keepdims=True)
    dx_ref[...] = norm_back(grad_h * gain_ref[...], normed, inv_std)

    @pl.when(step == pl.num_programs(0) - 1)
    def _():
        gwi_p[...] = acc_ip[...].astype(BF16)
        gwo_p[...] = acc_op[...].astype(BF16)


def mlp_branch(x_seq, go_seq, wi_o, wi_p, wo_o, wo_p, b_in, gain, bias):
    rows, width = x_seq.shape
    half, hid = wi_o.shape

    def whole(a):
        return pl.BlockSpec(a.shape, lambda i: (0,) * a.ndim)

    row_spec = pl.BlockSpec((BLOCK, width), lambda i: (i, 0))

    def shape(s, d):
        return jax.ShapeDtypeStruct(s, d)

    outs = [
        shape((rows, width), F32),
        shape((rows, width), F32),
        shape((half, hid), F32),
        shape((half, hid), BF16),
        shape((hid, half), F32),
        shape((hid, half), BF16),
        shape((8, width), F32),
    ]
    return pl.pallas_call(
        mlp_kernel,
        grid=(rows // BLOCK,),
        in_specs=[row_spec, row_spec]
        + [whole(a) for a in (wi_o, wi_p, wo_o, wo_p, b_in, gain, bias)],
        out_specs=[row_spec, row_spec] + [whole(a) for a in outs[2:]],
        out_shape=outs,
        scratch_shapes=[pltpu.VMEM((half, hid), F32), pltpu.VMEM((hid, half), F32)],
        compiler_params=pltpu.CompilerParams(
            dimension_semantics=("arbitrary",), vmem_limit_bytes=48 * 1024 * 1024
        ),
        cost_estimate=pl.CostEstimate(
            flops=12 * rows * width * hid, transcendentals=2 * rows * hid,
            bytes_accessed=24 * 1024 * 1024,
        ),
        name="mlp_branch",
    )(x_seq, go_seq, wi_o, wi_p, wo_o, wo_p, b_in, gain, bias)


def attn_kernel(
    x_ref, go_ref, w_ref, b_ref, wd_ref, cos_ref, s1_ref, s2_ref, segc_ref, segr_ref,
    gain_ref, bias_ref, mix_in, dx_in,
    mix_ref, dx_ref, gw_ref, gb_ref, gwd_ref, vec_ref,
    h_ref, mix_acc, dh_acc, qk_ref, v_ref, dctx_ref, ctxt_ref, dqt_ref, dk_ref, dv_ref, dj_ref,
):
    head = pl.program_id(0)
    last = pl.num_programs(0) - 1
    rows = x_ref.shape[0]
    tiles = rows // BLOCK

    @pl.when(head == 0)
    def _():
        @pl.loop(0, tiles)
        def _(t):
            at = pl.ds(t * BLOCK, BLOCK)
            normed, _ = normalize(x_ref[at, :])
            h_ref[at, :] = (normed * gain_ref[...] + bias_ref[...]).astype(BF16)

    lanes = lax.broadcasted_iota(jnp.int32, (1, 2 * HEAD_DIM), 1)
    scale = jnp.where(lanes < HEAD_DIM, HEAD_DIM ** (-0.5), 1.0)

    @pl.loop(0, tiles)
    def _(t):
        at = pl.ds(t * BLOCK, BLOCK)
        joined = dot_nn(h_ref[at, :], w_ref[0]) + b_ref[0]
        u = joined[:, : 2 * HEAD_DIM]
        turned = (
            u * cos_ref[at, :]
            + pltpu.roll(u, 2 * HEAD_DIM - ROT // 2, 1) * s1_ref[at, :]
            + pltpu.roll(u, ROT // 2, 1) * s2_ref[at, :]
        )
        qk_ref[at, :] = (turned * scale).astype(BF16)
        v_ref[at, :] = joined[:, 2 * HEAD_DIM :].astype(BF16)
        dctx_ref[at, :] = dot_nt(go_ref[at, :], wd_ref[0]).astype(BF16)

    qk_all = qk_ref[...]
    k_all = qk_all[:, HEAD_DIM:]
    kt = k_all.astype(F32).T.astype(BF16)
    vt = v_ref[...].astype(F32).T.astype(BF16)
    for i in range(tiles):
        lo = i * BLOCK
        hi = lo + BLOCK
        q_blk = qk_ref[lo:hi, :HEAD_DIM]
        g_blk = dctx_ref[lo:hi, :]
        st = dot_nt(k_all[:hi], q_blk)
        key_at = lax.broadcasted_iota(jnp.int32, (hi, BLOCK), 0)
        query_at = lax.broadcasted_iota(jnp.int32, (hi, BLOCK), 1) + lo
        allowed = (segc_ref[0:hi, :] == segr_ref[:, lo:hi]) & (key_at <= query_at)
        st = jnp.where(allowed, st, -1e30)
        top = jnp.max(st, axis=0, keepdims=True)
        p = jnp.exp(st - top)
        p = p * (1.0 / jnp.sum(p, axis=0, keepdims=True))
        pb = p.astype(BF16)
        ctxt_ref[:, lo:hi] = dot_nn(vt[:, :hi], pb).astype(BF16)
        dpt = dot_nt(v_ref[0:hi, :], g_blk)
        inner = jnp.sum(dpt * p, axis=0, keepdims=True)
        dst = (p * (dpt - inner)).astype(BF16)
        dqt_ref[:, lo:hi] = dot_nn(kt[:, :hi], dst)
        dk_new = dot_nn(dst, q_blk)
        dv_new = dot_nn(pb, g_blk)
        if i > 0:
            dk_ref[0:lo, :] += dk_new[:lo]
            dv_ref[0:lo, :] += dv_new[:lo]
        dk_ref[lo:hi, :] = dk_new[lo:]
        dv_ref[lo:hi, :] = dv_new[lo:]

    gwd_ref[0] = dot_nn(ctxt_ref[...], go_ref[...])
    dq = dqt_ref[...].T
    back = jnp.concatenate([dq * HEAD_DIM ** (-0.5), dk_ref[...]], axis=1)
    turned_back = (
        back * cos_ref[...]
        + pltpu.roll(back * s2_ref[...], 2 * HEAD_DIM - ROT // 2, 1)
        + pltpu.roll(back * s1_ref[...], ROT // 2, 1)
    )
    dj_ref[:, : 2 * HEAD_DIM] = turned_back.astype(BF16)
    dj_ref[:, 2 * HEAD_DIM :] = dv_ref[...].astype(BF16)
    gb_ref[0] = jnp.sum(dj_ref[...].astype(F32), axis=0, keepdims=True)

    for j in range(3):
        at = slice(j * BLOCK, (j + 1) * BLOCK)
        gw_ref[0, at, :] = dot_tn(h_ref[:, at], dj_ref[...])

    first = head == 0
    for t in range(tiles):
        at = slice(t * BLOCK, (t + 1) * BLOCK)
        dh_new = dot_nt(dj_ref[at, :], w_ref[0])
        mix_new = dot_tn(ctxt_ref[:, at], wd_ref[0])

        @pl.when(first)
        def _():
            dh_acc[at, :] = dh_new
            mix_acc[at, :] = mix_in[at, :] + mix_new

        @pl.when(head > 0)
        def _():
            dh_acc[at, :] += dh_new
            mix_acc[at, :] += mix_new

    @pl.when(head == last)
    def _():
        vec_ref[...] = jnp.zeros_like(vec_ref)

        @pl.loop(0, tiles)
        def _(t):
            at = pl.ds(t * BLOCK, BLOCK)
            normed, inv_std = normalize(x_ref[at, :])
            dh = dh_acc[at, :]
            vec_ref[0:1, :] += jnp.sum(dh * normed, axis=0, keepdims=True)
            vec_ref[1:2, :] += jnp.sum(dh, axis=0, keepdims=True)
            dx = norm_back(dh * gain_ref[...], normed, inv_std)
            dx_ref[at, :] = (dx_in[at, :] + dx).astype(BF16)
            mix_ref[at, :] = mix_acc[at, :].astype(BF16)


def attn_branch(x_seq, go_seq, w_heads, b_heads, wd_heads, tables, segc, segr, gain, bias, mix, dx):
    rows, width = x_seq.shape
    heads = w_heads.shape[0]
    inner = w_heads.shape[2]

    def whole(a):
        return pl.BlockSpec(a.shape, lambda i: (0,) * a.ndim)

    def per_head(a):
        return pl.BlockSpec((1,) + a.shape[1:], lambda i: (i,) + (0,) * (a.ndim - 1))

    def shape(s, d):
        return jax.ShapeDtypeStruct(s, d)

    outs = [
        shape((rows, width), BF16),
        shape((rows, width), BF16),
        shape((heads, width, inner), F32),
        shape((heads, 1, inner), F32),
        shape((heads, HEAD_DIM, width), F32),
        shape((8, width), F32),
    ]
    args = (x_seq, go_seq, w_heads, b_heads, wd_heads) + tables + (segc, segr, gain, bias, mix, dx)
    specs = [whole(a) for a in args]
    for j in (2, 3, 4):
        specs[j] = per_head(args[j])
    return pl.pallas_call(
        attn_kernel,
        grid=(heads,),
        in_specs=specs,
        out_specs=[whole(outs[0]), whole(outs[1])]
        + [per_head(a) for a in outs[2:5]]
        + [whole(outs[5])],
        out_shape=outs,
        scratch_shapes=[
            pltpu.VMEM((rows, width), BF16),
            pltpu.VMEM((rows, width), F32),
            pltpu.VMEM((rows, width), F32),
            pltpu.VMEM((rows, 2 * HEAD_DIM), BF16),
            pltpu.VMEM((rows, HEAD_DIM), BF16),
            pltpu.VMEM((rows, HEAD_DIM), BF16),
            pltpu.VMEM((HEAD_DIM, rows), BF16),
            pltpu.VMEM((HEAD_DIM, rows), F32),
            pltpu.VMEM((rows, HEAD_DIM), F32),
            pltpu.VMEM((rows, HEAD_DIM), F32),
            pltpu.VMEM((rows, inner), BF16),
        ],
        compiler_params=pltpu.CompilerParams(
            dimension_semantics=("arbitrary",), vmem_limit_bytes=56 * 1024 * 1024
        ),
        cost_estimate=pl.CostEstimate(
            flops=20 * 1000 * 1000 * 1000, transcendentals=heads * rows * rows,
            bytes_accessed=24 * 1024 * 1024,
        ),
        name="attn_branch",
    )(*args)


def group_perm(n_row, n_col, target):
    pairs = []
    for r in range(n_row):
        for c in range(n_col):
            to = target(r, c // 2, c % 2)
            if to is not None:
                pairs.append((r * n_col + c, to[0] * n_col + 2 * to[1] + to[2]))
    return pairs


def swap_row(value):
    return lax.ppermute(value, "row", [(0, 1), (1, 0)])


def dp_total(value):
    n_dp = lax.axis_size("dp")
    if n_dp != 4:
        return lax.psum(value, "dp")
    place = lax.axis_index("dp")
    inward = lax.ppermute(value.astype(BF16), "dp", [(0, 1), (3, 2)])
    pair = (value + inward.astype(F32)).astype(BF16)
    other = lax.ppermute(pair, "dp", [(1, 2), (2, 1)])
    total = (pair.astype(F32) + other.astype(F32)).astype(BF16)
    outward = lax.ppermute(total, "dp", [(1, 0), (2, 3)])
    return jnp.where((place == 1) | (place == 2), total, outward).astype(F32)


def swap_sum(value, axis, size, bit):
    return value + lax.ppermute(value, axis, [(i, i ^ bit) for i in range(size)])


def local(
    block_input, w_qkv, b_qkv, w_in, b_in, w_dense, b_dense, w_out, b_out,
    ln_attn_gain, ln_attn_bias, ln_mlp_gain, ln_mlp_bias, segments, positions, d_out,
):
    n_row = lax.axis_size("row")
    n_col = lax.axis_size("col")
    n_dp = lax.axis_size("dp")
    row = lax.axis_index("row")
    col = lax.axis_index("col")
    own_rows, half = block_input.shape
    upper = col // 2
    core = col % 2
    home = row == upper
    heads = w_qkv.shape[1] // (3 * HEAD_DIM)

    spread = group_perm(
        n_row, n_col, lambda r, u, k: (r, 1 - u, k) if r == u else (1 - r, u, k)
    )
    cross = group_perm(n_row, n_col, lambda r, u, k: None if r == u else (1 - r, 1 - u, k))
    pair = group_perm(n_row, n_col, lambda r, u, k: (r, u, 1 - k))
    collect = group_perm(
        n_row, n_col, lambda r, u, k: (1 - r, u, k) if r == u else (r, 1 - u, k)
    )

    def gather_seq(block):
        near = lax.ppermute(block, GROUP, spread)
        far = lax.ppermute(block, GROUP, cross)
        mine = jnp.concatenate(
            [jnp.where(home, block, near), jnp.where(home, near, far)], axis=1
        )
        other = lax.ppermute(mine, GROUP, pair)
        return jnp.where(
            core == 0,
            jnp.concatenate([mine, other], axis=0),
            jnp.concatenate([other, mine], axis=0),
        )

    def reduce_seq(part):
        low = part[:own_rows]
        high = part[own_rows:]
        got = lax.ppermute(jnp.where(core == 0, high, low), GROUP, pair)
        kept = jnp.where(core == 0, low, high)
        summed = kept.astype(F32) + got.astype(F32)
        low_sum = summed.astype(BF16)
        near = lax.ppermute(
            jnp.where(home, low_sum[:, half:], low_sum[:, :half]), GROUP, collect
        )
        far = lax.ppermute(low_sum[:, half:], GROUP, cross)
        return near.astype(F32) + jnp.where(home, summed[:, :half], far.astype(F32))

    norms = jnp.stack([ln_attn_gain, ln_attn_bias, ln_mlp_gain, ln_mlp_bias])
    norms = jnp.concatenate([norms, swap_row(norms)], axis=1)
    x_seq = gather_seq(block_input)
    wi_p = swap_row(w_in)
    go_seq = gather_seq(d_out)
    wo_p = swap_row(w_out)
    wq_p = swap_row(w_qkv)
    wd_p = swap_row(w_dense)

    at_seq = row * SEQ_LEN
    seg_seq = lax.dynamic_slice_in_dim(segments, at_seq, SEQ_LEN)
    pos_seq = lax.dynamic_slice_in_dim(positions, at_seq, SEQ_LEN)
    lane = jnp.arange(2 * HEAD_DIM) % HEAD_DIM
    freq_steps = (lane % (ROT // 2)).astype(F32) * (-2.0 * math.log(10000.0) / ROT)
    freq = jnp.where(lane < ROT, jnp.exp(freq_steps), 0.0)
    angles = pos_seq.astype(F32)[:, None] * freq[None, :]
    cos_table = jnp.cos(angles)
    sin_table = jnp.sin(angles)
    sin_up = jnp.where(lane < ROT // 2, -sin_table, 0.0)
    sin_down = jnp.where((lane >= ROT // 2) & (lane < ROT), sin_table, 0.0)

    w_heads = jnp.concatenate([w_qkv, wq_p], axis=0).reshape(D, heads, 3 * HEAD_DIM)
    w_heads = w_heads.transpose(1, 0, 2)
    wd_heads = jnp.concatenate([w_dense, wd_p], axis=1).reshape(heads, HEAD_DIM, D)

    mix, dx, gwi_o, gwi_p, gwo_o, gwo_p, mlp_vec = mlp_branch(
        x_seq, go_seq, w_in, wi_p, w_out, wo_p, b_in[None], norms[2:3], norms[3:4]
    )
    grad_w_in = dp_total(gwi_o + swap_row(gwi_p).astype(F32))
    grad_w_out = dp_total(gwo_o + swap_row(gwo_p).astype(F32))

    mix, dx, gw_heads, gb_heads, gwd, attn_vec = attn_branch(
        x_seq, go_seq, w_heads, b_qkv.reshape(heads, 1, 3 * HEAD_DIM), wd_heads,
        (cos_table, sin_up, sin_down), seg_seq[:, None], seg_seq[None, :],
        norms[0:1], norms[1:2], mix, dx,
    )
    gw = gw_heads.transpose(1, 0, 2).reshape(D, w_qkv.shape[1])
    grad_w_qkv = dp_total(gw[:half] + swap_row(gw[half:].astype(BF16)).astype(F32))
    gwd = gwd.reshape(w_dense.shape[0], D)
    grad_w_dense = dp_total(gwd[:, :half] + swap_row(gwd[:, half:].astype(BF16)).astype(F32))

    block_output = (
        block_input.astype(F32) + reduce_seq(mix) + b_dense + b_out
    ).astype(BF16)
    d_out_f = d_out.astype(F32)
    d_input = d_out_f + reduce_seq(dx)

    feature_vecs = jnp.concatenate([attn_vec[:2], mlp_vec[:2]], axis=0)
    wide = jnp.concatenate([mlp_vec[2], gb_heads.reshape(-1)])
    mine = jnp.concatenate([feature_vecs[:, :half].reshape(-1), wide])
    theirs = jnp.concatenate([feature_vecs[:, half:].reshape(-1), wide])
    vecs = mine + swap_row(theirs)
    vecs = jnp.concatenate([vecs, jnp.sum(d_out_f, axis=0)])
    if n_dp == 4:
        vecs = swap_sum(vecs, "dp", 4, 1)
        vecs = swap_sum(vecs, "dp", 4, 2)
    else:
        vecs = lax.psum(vecs, "dp")
    hid = b_in.shape[0]
    width = b_qkv.shape[0]
    at_in = 4 * half
    at_qkv = at_in + hid
    at_out = at_qkv + width
    grad_b_in = vecs[at_in:at_qkv]
    grad_b_qkv = vecs[at_qkv:at_out]
    rest = jnp.concatenate([vecs[:at_in], vecs[at_out:]])
    rest = swap_sum(rest, "col", n_col, 1)
    rest = swap_sum(rest, "col", n_col, 2)
    rest = rest.reshape(5, half)
    return (
        block_output, d_input, grad_w_qkv, grad_b_qkv, grad_w_in, grad_b_in,
        grad_w_dense, rest[4], grad_w_out, rest[4], rest[0], rest[1], rest[2], rest[3],
    )


def solution(mesh):
    token = P(("dp", "col"), "row")
    placed = (
        token, P("row", "col"), P("col"), P("row", "col"), P("col"), P("col", "row"), P("row"),
        P("col", "row"), P("row"), P("row"), P("row"), P("row"), P("row"), P("dp"), P("dp"), token,
    )
    return jax.shard_map(
        local,
        mesh=mesh,
        in_specs=placed,
        out_specs=(
            token, token, P("row", "col"), P("col"), P("row", "col"), P("col"), P("col", "row"),
            P("row"), P("col", "row"), P("row"), P("row"), P("row"), P("row"), P("row"),
        ),
        check_vma=False,
    )
```

```python
import math

import jax
import jax.numpy as jnp
from jax import lax
from jax.experimental import pallas as pl
from jax.experimental.pallas import tpu as pltpu
from jax.sharding import PartitionSpec as P

D = 768
HEAD_DIM = 64
ROT = 16
SEQ_LEN = 1024
EPSILON = 1e-05
BLOCK = 256
F32 = jnp.float32
BF16 = jnp.bfloat16
GROUP = ("row", "col")
VMEM_BYTES = 60 * 1024 * 1024


def dot_nn(a, b):
    return lax.dot_general(a, b, (((1,), (0,)), ((), ())), preferred_element_type=F32)


def dot_tn(a, b):
    return lax.dot_general(a, b, (((0,), (0,)), ((), ())), preferred_element_type=F32)


def dot_nt(a, b):
    return lax.dot_general(a, b, (((1,), (1,)), ((), ())), preferred_element_type=F32)


def normalize(x_rows):
    x = x_rows.astype(F32)
    mean = jnp.mean(x, axis=1, keepdims=True)
    centered = x - mean
    var = jnp.mean(centered * centered, axis=1, keepdims=True)
    inv_std = lax.rsqrt(var + EPSILON)
    return centered * inv_std, inv_std


def norm_back(grad, normed, inv_std):
    mean_grad = jnp.mean(grad, axis=1, keepdims=True)
    mean_cross = jnp.mean(grad * normed, axis=1, keepdims=True)
    return inv_std * (grad - mean_grad - normed * mean_cross)


def mlp_part(x_rows, go, wi_o, wi_p, wo_o, wo_p, b_ref, gain_ref, bias_ref, own_ref, send_acc):
    half = wi_o.shape[0]
    normed, _ = normalize(x_rows)
    h = (normed * gain_ref[...] + bias_ref[...]).astype(BF16)
    pre = dot_nn(h[:, :half], wi_o[...]) + dot_nn(h[:, half:], wi_p[...]) + b_ref[...]
    cdf = 0.5 * (1.0 + lax.erf(pre * (2.0 ** -0.5)))
    hidden = (pre * cdf).astype(BF16)
    slope = cdf + pre * (jnp.exp(-0.5 * pre * pre) * (1.0 / math.sqrt(2.0 * math.pi)))
    mix = jnp.concatenate([dot_nn(hidden, wo_o[...]), dot_nn(hidden, wo_p[...])], axis=1)
    grad_hidden = dot_nt(go[:, :half], wo_o[...]) + dot_nt(go[:, half:], wo_p[...])
    grad_pre = (grad_hidden * slope).astype(BF16)
    own_ref[:half, :] += dot_tn(h[:, :half], grad_pre)
    send_acc[:half, :] += dot_tn(h[:, half:], grad_pre)
    own_ref[half:, :] += dot_tn(hidden, go[:, :half])
    send_acc[half:, :] += dot_tn(hidden, go[:, half:])
    grad_h = jnp.concatenate([dot_nt(grad_pre, wi_o[...]), dot_nt(grad_pre, wi_p[...])], axis=1)
    return normed, mix, grad_h, jnp.sum(grad_pre.astype(F32), axis=0, keepdims=True)


def mlp_first_kernel(
    core_ref, xm_ref, xo_ref, gm_ref, go_ref, wi_o, wo_o, wi_p, wo_p, b_ref, gain_ref, bias_ref,
    again_ref, abias_ref,
    mix_ref, gh_ref, x_out, go_out, h_out, own_ref, send_ref, gb_ref,
    own_acc, acc_ref,
):
    step = pl.program_id(0)

    @pl.when(step == 0)
    def _():
        own_acc[...] = jnp.zeros_like(own_acc)
        acc_ref[...] = jnp.zeros_like(acc_ref)
        gb_ref[...] = jnp.zeros_like(gb_ref)

    held = step // (pl.num_programs(0) // 2) == core_ref[0]
    x_rows = jnp.where(held, xm_ref[...], xo_ref[...])
    go = jnp.where(held, gm_ref[...], go_ref[...])
    x_out[...] = x_rows
    go_out[...] = go
    normed, mix, grad_h, gb = mlp_part(
        x_rows, go, wi_o, wi_p, wo_o, wo_p, b_ref, gain_ref, bias_ref, own_acc, acc_ref
    )
    h_out[...] = (normed * again_ref[...] + abias_ref[...]).astype(BF16)
    mix_ref[...] = mix
    gh_ref[...] = grad_h
    gb_ref[0:1, :] += gb

    @pl.when(step == pl.num_programs(0) - 1)
    def _():
        own_ref[...] = own_acc[...].astype(BF16)
        send_ref[...] = acc_ref[...].astype(BF16)


def mlp_second_kernel(
    x_ref, go_ref, mix_in, gh_in, wi_o, wo_o, wi_p, wo_p, b_ref, gain_ref, bias_ref,
    mix_ref, gh_ref, own_ref, send_ref, gb_ref,
    own_acc, acc_ref,
):
    step = pl.program_id(0)

    @pl.when(step == 0)
    def _():
        own_acc[...] = jnp.zeros_like(own_acc)
        acc_ref[...] = jnp.zeros_like(acc_ref)
        gb_ref[...] = jnp.zeros_like(gb_ref)

    _, mix, grad_h, gb = mlp_part(
        x_ref[...], go_ref[...], wi_o, wi_p, wo_o, wo_p, b_ref, gain_ref, bias_ref, own_acc, acc_ref
    )
    mix_ref[...] = mix_in[...] + mix
    gh_ref[...] = gh_in[...] + grad_h
    gb_ref[0:1, :] += gb

    @pl.when(step == pl.num_programs(0) - 1)
    def _():
        own_ref[...] = own_acc[...].astype(BF16)
        send_ref[...] = acc_ref[...].astype(BF16)


def brief():
    return pl.CostEstimate(flops=1024, transcendentals=0, bytes_accessed=1024)


def whole(a):
    return pl.BlockSpec(a.shape, lambda *i: (0,) * a.ndim)


def shape(s, d):
    return jax.ShapeDtypeStruct(s, d)


def mlp_params():
    return pltpu.CompilerParams(
        dimension_semantics=("arbitrary",), vmem_limit_bytes=VMEM_BYTES
    )


def part_spec(size, at):
    return pl.BlockSpec((size, size), lambda *i: at)


def mlp_first(core, x_mine, x_other, go_mine, go_other, w_in, w_out, pack, b_in, *norms):
    held, width = x_mine.shape
    rows = 2 * held
    half = width // 2
    steps = held // BLOCK

    def held_map(i, core_ref):
        return (jnp.clip(i - core_ref[0] * steps, 0, steps - 1), 0)

    def other_map(i, core_ref):
        return (jnp.clip(i - (1 - core_ref[0]) * steps, 0, steps - 1), 0)

    mine_spec = pl.BlockSpec((BLOCK, width), held_map)
    other_spec = pl.BlockSpec((BLOCK, width), other_map)
    row_spec = pl.BlockSpec((BLOCK, width), lambda i, core_ref: (i, 0))
    outs = [
        shape((rows, width), F32),
        shape((rows, width), F32),
        shape((rows, width), BF16),
        shape((rows, width), BF16),
        shape((rows, width), BF16),
        shape((2 * half, half), BF16),
        shape((2 * half, half), BF16),
        shape((8, half), F32),
    ]
    return pl.pallas_call(
        mlp_first_kernel,
        grid_spec=pltpu.PrefetchScalarGridSpec(
            num_scalar_prefetch=1,
            grid=(rows // BLOCK,),
            in_specs=[mine_spec, other_spec, mine_spec, other_spec]
            + [part_spec(half, (0, 0)), part_spec(half, (0, 0))]
            + [part_spec(half, (0, 0)), part_spec(half, (1, 0))]
            + [pl.BlockSpec((1, half), lambda *i: (0, 0))]
            + [whole(a) for a in norms],
            out_specs=[row_spec] * 5 + [whole(a) for a in outs[5:]],
            scratch_shapes=[pltpu.VMEM((2 * half, half), F32)] * 2,
        ),
        out_shape=outs,
        compiler_params=mlp_params(),
        cost_estimate=brief(),
        name="mlp_first",
    )(core, x_mine, x_other, go_mine, go_other, w_in, w_out, pack, pack, b_in, *norms)


def mlp_second(x_seq, go_seq, mix, gh, w_in, w_out, pack, b_in, *norms):
    rows, width = x_seq.shape
    half = width // 2
    row_spec = pl.BlockSpec((BLOCK, width), lambda i: (i, 0))
    outs = [
        shape((rows, width), F32),
        shape((rows, width), F32),
        shape((2 * half, half), BF16),
        shape((2 * half, half), BF16),
        shape((8, half), F32),
    ]
    return pl.pallas_call(
        mlp_second_kernel,
        grid=(rows // BLOCK,),
        in_specs=[row_spec] * 4
        + [part_spec(half, (0, 1)), part_spec(half, (1, 0))]
        + [part_spec(half, (0, 0)), part_spec(half, (1, 0))]
        + [pl.BlockSpec((1, half), lambda *i: (0, 1))]
        + [whole(a) for a in norms],
        out_specs=[row_spec] * 2 + [whole(a) for a in outs[2:]],
        out_shape=outs,
        scratch_shapes=[pltpu.VMEM((2 * half, half), F32)] * 2,
        compiler_params=mlp_params(),
        cost_estimate=brief(),
        name="mlp_second",
    )(x_seq, go_seq, mix, gh, w_in, w_out, pack, pack, b_in, *norms)


def attn_kernel(
    h_ref, go_ref, wo_ref, wp_ref, b_ref, do_ref, dp_ref, cos_ref, s1_ref, s2_ref,
    segc_ref, segr_ref,
    ctx_out, dj_out, own_ref, send_ref, gb_ref,
    qk_ref, v_ref, dctx_ref, ctxt_ref, dqt_ref, dk_ref, dv_ref,
):
    rows = h_ref.shape[0]
    inner, half = wo_ref.shape
    tiles = rows // BLOCK
    lanes = lax.broadcasted_iota(jnp.int32, (1, 2 * HEAD_DIM), 1)
    scale = jnp.where(lanes < HEAD_DIM, HEAD_DIM ** (-0.5), 1.0)

    for t in range(tiles):
        at = slice(t * BLOCK, (t + 1) * BLOCK)
        joined = (
            dot_nt(h_ref[at, :half], wo_ref[...]) + dot_nt(h_ref[at, half:], wp_ref[...]) + b_ref[0]
        )
        u = joined[:, : 2 * HEAD_DIM]
        turned = (
            u * cos_ref[at, :]
            + pltpu.roll(u, 2 * HEAD_DIM - ROT // 2, 1) * s1_ref[at, :]
            + pltpu.roll(u, ROT // 2, 1) * s2_ref[at, :]
        )
        qk_ref[at, :] = (turned * scale).astype(BF16)
        v_ref[at, :] = joined[:, 2 * HEAD_DIM :].astype(BF16)
        dctx_ref[at, :] = (
            dot_nt(go_ref[at, :half], do_ref[...]) + dot_nt(go_ref[at, half:], dp_ref[...])
        ).astype(BF16)

    k_all = qk_ref[:, HEAD_DIM:]
    kt = k_all.astype(F32).T.astype(BF16)
    vt = v_ref[...].astype(F32).T.astype(BF16)
    for i in range(tiles):
        lo = i * BLOCK
        hi = lo + BLOCK
        q_blk = qk_ref[lo:hi, :HEAD_DIM]
        g_blk = dctx_ref[lo:hi, :]
        st = dot_nt(k_all[:hi], q_blk)
        key_at = lax.broadcasted_iota(jnp.int32, (hi, BLOCK), 0)
        query_at = lax.broadcasted_iota(jnp.int32, (hi, BLOCK), 1) + lo
        allowed = (segc_ref[0:hi, :] == segr_ref[:, lo:hi]) & (key_at <= query_at)
        st = jnp.where(allowed, st, -1e30)
        top = jnp.max(st, axis=0, keepdims=True)
        p = jnp.exp(st - top)
        p = p * (1.0 / jnp.sum(p, axis=0, keepdims=True))
        pb = p.astype(BF16)
        ctxt_ref[:, lo:hi] = dot_nn(vt[:, :hi], pb).astype(BF16)
        dpt = dot_nt(v_ref[0:hi, :], g_blk)
        inner_term = jnp.sum(dpt * p, axis=0, keepdims=True)
        dst = (p * (dpt - inner_term)).astype(BF16)
        dqt_ref[:, lo:hi] = dot_nn(kt[:, :hi], dst)
        dk_new = dot_nn(dst, q_blk)
        dv_new = dot_nn(pb, g_blk)
        if i > 0:
            dk_ref[0:lo, :] += dk_new[:lo]
            dv_ref[0:lo, :] += dv_new[:lo]
        dk_ref[lo:hi, :] = dk_new[lo:]
        dv_ref[lo:hi, :] = dv_new[lo:]

    ctx_out[0] = ctxt_ref[...]
    dq = dqt_ref[...].T
    back = jnp.concatenate([dq * HEAD_DIM ** (-0.5), dk_ref[...]], axis=1)
    turned_back = (
        back * cos_ref[...]
        + pltpu.roll(back * s2_ref[...], 2 * HEAD_DIM - ROT // 2, 1)
        + pltpu.roll(back * s1_ref[...], ROT // 2, 1)
    )
    dj = jnp.concatenate([turned_back.astype(BF16), dv_ref[...].astype(BF16)], axis=1)
    dj_out[0] = dj
    gb_ref[0] = jnp.sum(dj.astype(F32), axis=0, keepdims=True)
    own_ref[0, :inner, :] = dot_tn(dj, h_ref[:, :half]).astype(BF16)
    own_ref[0, inner:, :] = dot_nn(ctxt_ref[...], go_ref[:, :half]).astype(BF16)
    send_ref[0, :inner, :] = dot_tn(dj, h_ref[:, half:]).astype(BF16)
    send_ref[0, inner:, :] = dot_nn(ctxt_ref[...], go_ref[:, half:]).astype(BF16)


def attn_head(first, count, h_seq, go_seq, wq_o, wq_p, b_heads, wd_o, wd_p, *tables):
    rows = h_seq.shape[0]
    half = wq_o.shape[1]
    inner = 3 * HEAD_DIM
    skip = wq_o.shape[0] // HEAD_DIM

    def per_head(a, base):
        return pl.BlockSpec((1,) + a.shape[1:], lambda i: (i + base,) + (0,) * (a.ndim - 1))

    outs = [
        shape((count, HEAD_DIM, rows), BF16),
        shape((count, rows, inner), BF16),
        shape((count, inner + HEAD_DIM, half), BF16),
        shape((count, inner + HEAD_DIM, half), BF16),
        shape((count, 1, inner), F32),
    ]
    args = (h_seq, go_seq, wq_o, wq_p, b_heads, wd_o, wd_p) + tables
    specs = [whole(a) for a in args]
    for j in (2, 3):
        specs[j] = pl.BlockSpec((inner, half), lambda i: (i + first, 0))
    specs[4] = per_head(b_heads, first)
    specs[5] = pl.BlockSpec((HEAD_DIM, half), lambda i: (i + first, 0))
    specs[6] = pl.BlockSpec((HEAD_DIM, half), lambda i: (i + first + skip, 0))
    return pl.pallas_call(
        attn_kernel,
        grid=(count,),
        in_specs=specs,
        out_specs=[per_head(a, 0) for a in outs],
        out_shape=outs,
        scratch_shapes=[
            pltpu.VMEM((rows, 2 * HEAD_DIM), BF16),
            pltpu.VMEM((rows, HEAD_DIM), BF16),
            pltpu.VMEM((rows, HEAD_DIM), BF16),
            pltpu.VMEM((HEAD_DIM, rows), BF16),
            pltpu.VMEM((HEAD_DIM, rows), F32),
            pltpu.VMEM((rows, HEAD_DIM), F32),
            pltpu.VMEM((rows, HEAD_DIM), F32),
        ],
        compiler_params=pltpu.CompilerParams(
            dimension_semantics=("arbitrary",), vmem_limit_bytes=VMEM_BYTES
        ),
        cost_estimate=brief(),
        name="attn_head",
    )(*args)


def close_kernel(
    core_ref, x_ref, mix_ref, gh_ref, c01, c2, j01, j2, wq_o, wq_p, wd_o, wd_p,
    again_ref, mgain_ref,
    mix_send, mix_keep, dx_send, dx_keep, vec_ref,
):
    del core_ref
    step = pl.program_id(0)
    sending = step < pl.num_programs(0) // 2

    @pl.when(step == 0)
    def _():
        vec_ref[...] = jnp.zeros_like(vec_ref)

    ctxt = jnp.concatenate([c01[0], c01[1], c2[0]], axis=0)
    mix = mix_ref[...] + jnp.concatenate(
        [dot_tn(ctxt, wd_o[...]), dot_tn(ctxt, wd_p[...])], axis=1
    )
    grad_h = jnp.concatenate(
        [
            sum(
                dot_nn(j, w[n * 3 * HEAD_DIM : (n + 1) * 3 * HEAD_DIM, :])
                for n, j in enumerate((j01[0], j01[1], j2[0]))
            )
            for w in (wq_o, wq_p)
        ],
        axis=1,
    )
    normed, inv_std = normalize(x_ref[...])
    vec_ref[0:1, :] += jnp.sum(grad_h * normed, axis=0, keepdims=True)
    vec_ref[1:2, :] += jnp.sum(grad_h, axis=0, keepdims=True)
    grad_m = gh_ref[...]
    vec_ref[2:3, :] += jnp.sum(grad_m * normed, axis=0, keepdims=True)
    vec_ref[3:4, :] += jnp.sum(grad_m, axis=0, keepdims=True)
    dx = norm_back(grad_h * again_ref[...] + grad_m * mgain_ref[...], normed, inv_std)

    @pl.when(sending)
    def _():
        mix_send[...] = mix.astype(BF16)
        dx_send[...] = dx.astype(BF16)

    @pl.when(jnp.logical_not(sending))
    def _():
        mix_keep[...] = mix.astype(BF16)
        dx_keep[...] = dx.astype(BF16)


def close_layer(core, x_seq, mix, gh, ctx, djs, *weights):
    rows, width = x_seq.shape
    held = rows // 2
    steps = held // BLOCK

    def block_of(i, core_ref):
        return jnp.where(i < steps, (1 - core_ref[0]) * steps + i, (core_ref[0] - 1) * steps + i)

    row_spec = pl.BlockSpec((BLOCK, width), lambda i, c: (block_of(i, c), 0))
    send_spec = pl.BlockSpec((BLOCK, width), lambda i, c: (jnp.minimum(i, steps - 1), 0))
    keep_spec = pl.BlockSpec((BLOCK, width), lambda i, c: (jnp.maximum(i - steps, 0), 0))
    ctx_specs = [
        pl.BlockSpec((a.shape[0], HEAD_DIM, BLOCK), lambda i, c: (0, 0, block_of(i, c)))
        for a in ctx
    ]
    dj_specs = [
        pl.BlockSpec((a.shape[0], BLOCK, 3 * HEAD_DIM), lambda i, c: (0, block_of(i, c), 0))
        for a in djs
    ]
    specs = [whole(a) for a in weights]
    wide, half = weights[0].shape
    deep = weights[2].shape[0]
    specs[1] = pl.BlockSpec((wide, half), lambda *i: (0, 0))
    specs[3] = pl.BlockSpec((deep, half), lambda *i: (wide // deep, 0))
    outs = [
        shape((held, width), BF16),
        shape((held, width), BF16),
        shape((held, width), BF16),
        shape((held, width), BF16),
        shape((8, width), F32),
    ]
    return pl.pallas_call(
        close_kernel,
        grid_spec=pltpu.PrefetchScalarGridSpec(
            num_scalar_prefetch=1,
            grid=(rows // BLOCK,),
            in_specs=[row_spec] * 3 + ctx_specs + dj_specs + specs,
            out_specs=[send_spec, keep_spec, send_spec, keep_spec, whole(outs[4])],
        ),
        out_shape=outs,
        compiler_params=pltpu.CompilerParams(
            dimension_semantics=("arbitrary",), vmem_limit_bytes=VMEM_BYTES
        ),
        cost_estimate=brief(),
        name="close_layer",
    )(core, x_seq, mix, gh, *ctx, *djs, *weights)


def group_perm(n_row, n_col, target):
    pairs = []
    for r in range(n_row):
        for c in range(n_col):
            to = target(r, c // 2, c % 2)
            if to is not None:
                pairs.append((r * n_col + c, to[0] * n_col + 2 * to[1] + to[2]))
    return pairs


def swap_row(value):
    return lax.ppermute(value, "row", [(0, 1), (1, 0)])


def dp_inward(value):
    return lax.ppermute(value, "dp", [(0, 1), (3, 2)])


def dp_middle(value, inward):
    pair = (value.astype(F32) + inward.astype(F32)).astype(BF16)
    return pair, lax.ppermute(pair, "dp", [(1, 2), (2, 1)])


def dp_outward(pair, other):
    total = (pair.astype(F32) + other.astype(F32)).astype(BF16)
    return total, lax.ppermute(total, "dp", [(1, 0), (2, 3)])


def dp_finish(total, outward=None):
    if outward is None:
        return total
    place = lax.axis_index("dp")
    return jnp.where((place == 1) | (place == 2), total, outward).astype(F32)


def swap_sum(value, axis, size, bit):
    return value + lax.ppermute(value, axis, [(i, i ^ bit) for i in range(size)])


def local(
    block_input, w_qkv, b_qkv, w_in, b_in, w_dense, b_dense, w_out, b_out,
    ln_attn_gain, ln_attn_bias, ln_mlp_gain, ln_mlp_bias, segments, positions, d_out,
):
    n_row = lax.axis_size("row")
    n_col = lax.axis_size("col")
    n_dp = lax.axis_size("dp")
    row = lax.axis_index("row")
    col = lax.axis_index("col")
    half = block_input.shape[1]
    barrier = lax.optimization_barrier
    upper = col // 2
    core = col % 2
    home = row == upper
    heads = w_qkv.shape[1] // (3 * HEAD_DIM)

    spread = group_perm(
        n_row, n_col, lambda r, u, k: (r, 1 - u, k) if r == u else (1 - r, u, k)
    )
    cross = group_perm(n_row, n_col, lambda r, u, k: None if r == u else (1 - r, 1 - u, k))
    pair = group_perm(n_row, n_col, lambda r, u, k: (r, u, 1 - k))
    forward = group_perm(n_row, n_col, lambda r, u, k: (r, 1 - u, k) if r == u else None)
    collect = group_perm(
        n_row, n_col, lambda r, u, k: (1 - r, u, k) if r == u else (r, 1 - u, k)
    )

    chain = n_dp == 4
    inner = 3 * HEAD_DIM
    wq_t = w_qkv.T
    pack_a = jnp.concatenate([w_in[:, :half], w_out[:half]], axis=0)
    pack_b = jnp.concatenate([w_in[:, half:], w_out[half:]], axis=0)
    pack_c = jnp.concatenate([wq_t, w_dense], axis=0)
    norms = jnp.stack([ln_attn_gain, ln_attn_bias, ln_mlp_gain, ln_mlp_bias])
    core_at = core.reshape(1)

    at_seq = row * SEQ_LEN
    seg_seq = lax.dynamic_slice_in_dim(segments, at_seq, SEQ_LEN)
    pos_seq = lax.dynamic_slice_in_dim(positions, at_seq, SEQ_LEN)
    lane = jnp.arange(2 * HEAD_DIM) % HEAD_DIM
    freq_steps = (lane % (ROT // 2)).astype(F32) * (-2.0 * math.log(10000.0) / ROT)
    freq = jnp.where(lane < ROT, jnp.exp(freq_steps), 0.0)
    angles = pos_seq.astype(F32)[:, None] * freq[None, :]
    cos_table = jnp.cos(angles)
    sin_table = jnp.sin(angles)
    sin_up = jnp.where(lane < ROT // 2, -sin_table, 0.0)
    sin_down = jnp.where((lane >= ROT // 2) & (lane < ROT), sin_table, 0.0)

    def join(block, near, far):
        return jnp.concatenate(
            [jnp.where(home, block, near), jnp.where(home, near, far)], axis=1
        )

    d_out_f = d_out.astype(F32)
    d_sum = jnp.sum(d_out_f, axis=0)
    norms_got = swap_row(norms)
    near_x = lax.ppermute(block_input, GROUP, spread)
    segc = seg_seq[:, None]
    go_in, cos_table, sin_up, sin_down, pack_a, pack_b, pack_c, segc, d_sum = barrier(
        (d_out, cos_table, sin_up, sin_down, pack_a, pack_b, pack_c, segc, d_sum)
    )
    near_go = lax.ppermute(go_in, GROUP, spread)
    near_x, norms, norms_got, pack_a = barrier((near_x, norms, norms_got, pack_a))
    far_x = lax.ppermute(near_x, GROUP, forward)
    got_a = swap_row(pack_a)
    far_go = lax.ppermute(near_go, GROUP, forward)
    x_mine = join(block_input, near_x, far_x)
    x_other = lax.ppermute(x_mine, GROUP, pair)
    far_go, got_a, pack_b = barrier((far_go, got_a, pack_b))
    go_mine = join(d_out, near_go, far_go)
    go_other = lax.ppermute(go_mine, GROUP, pair)
    got_b = swap_row(pack_b)
    x_other, pack_c = barrier((x_other, pack_c))
    got_c = swap_row(pack_c)
    norms = jnp.concatenate([norms, norms_got], axis=1)

    mix, gh, x_seq, go_seq, h_seq, own_a, send_a, gb_a = mlp_first(
        core_at, x_mine, x_other, go_mine, go_other, w_in, w_out, got_a, b_in[None],
        norms[2:3], norms[3:4], norms[0:1], norms[1:2],
    )
    x_seq, send_a = barrier((x_seq, send_a))
    back_a = swap_row(send_a)
    mix, gh, own_b, send_b, gb_b = mlp_second(
        x_seq, go_seq, mix, gh, w_in, w_out, got_b, b_in[None], norms[2:3], norms[3:4]
    )
    h_seq, send_b, got_c = barrier((h_seq, send_b, got_c))
    back_b = swap_row(send_b)
    width = wq_t.shape[0]
    heads_args = (
        wq_t, got_c, b_qkv.reshape(heads, 1, inner), w_dense, got_c,
        cos_table, sin_up, sin_down, segc, seg_seq[None, :],
    )

    def payload_sum(own, got):
        return (own.astype(F32) + got.astype(F32)).astype(BF16)

    heads01 = attn_head(0, heads - 1, h_seq, go_seq, *heads_args)
    go_seq, heads01, back_a = barrier((go_seq, heads01, back_a))
    back01 = swap_row(heads01[3])
    sum_a = payload_sum(own_a, back_a)
    if chain:
        in_a = dp_inward(sum_a)
    head2 = attn_head(heads - 1, 1, h_seq, go_seq, *heads_args)
    x_seq, head2, back_b = barrier((x_seq, head2, back_b))
    back2 = swap_row(head2[3])
    sum_b = payload_sum(own_b, back_b)
    if chain:
        in_b = dp_inward(sum_b)
    done = [heads01, head2]
    mix_s, mix_k, dx_s, dx_k, attn_vec = close_layer(
        core_at, x_seq, mix, gh, [a[0] for a in done], [a[1] for a in done],
        wq_t, got_c, w_dense, got_c, norms[0:1], norms[2:3],
    )
    if chain:
        mix_s, dx_s, in_a, sum_a, back01 = barrier((mix_s, dx_s, in_a, sum_a, back01))
        pair_a, other_a = dp_middle(sum_a, in_a)
    mix_got = lax.ppermute(mix_s, GROUP, pair)
    dx_got = lax.ppermute(dx_s, GROUP, pair)
    sum_c = payload_sum(heads01[2], back01).reshape(-1, half)
    if chain:
        in_c = dp_inward(sum_c)
    hid = b_in.shape[0]
    wide = jnp.concatenate([gb_a[0], gb_b[0]] + [a[4].reshape(-1) for a in done])
    mine = jnp.concatenate([attn_vec[:4, :half].reshape(-1), wide])
    theirs = jnp.concatenate([attn_vec[:4, half:].reshape(-1), wide])
    vec_got = swap_row(theirs)
    mix_got, dx_got, back2 = barrier((mix_got, dx_got, back2))
    sum_d = payload_sum(head2[2], back2).reshape(-1, half)
    if chain:
        in_d = dp_inward(sum_d)

    def reduce_start(got, kept):
        low_sum = (kept.astype(F32) + got.astype(F32)).astype(BF16)
        near = lax.ppermute(
            jnp.where(home, low_sum[:, half:], low_sum[:, :half]), GROUP, collect
        )
        return near, lax.ppermute(low_sum[:, half:], GROUP, cross), low_sum[:, :half]

    def reduce_end(near, far, kept):
        return near.astype(F32) + jnp.where(home, kept, far).astype(F32)

    mix_parts = reduce_start(mix_got, mix_k)
    dx_parts = reduce_start(dx_got, dx_k)
    vecs = mine + vec_got
    wide = vecs[4 * half :]
    rest = jnp.concatenate([vecs[: 4 * half], d_sum])
    rest = swap_sum(rest, "col", n_col, 1)
    rest = swap_sum(rest, "col", n_col, 2)
    vecs = jnp.concatenate([rest, wide])
    if chain:
        in_b, sum_b, other_a = barrier((in_b, sum_b, other_a))
        pair_b, other_b = dp_middle(sum_b, in_b)
        totals_a = dp_outward(pair_a, other_a)
        in_c, sum_c, in_d, sum_d = barrier((in_c, sum_c, in_d, sum_d))
        pair_c, other_c = dp_middle(sum_c, in_c)
        pair_d, other_d = dp_middle(sum_d, in_d)
        mix_parts, dx_parts, vecs, other_b = barrier((mix_parts, dx_parts, vecs, other_b))
        totals_b = dp_outward(pair_b, other_b)
        vecs = swap_sum(vecs, "dp", 4, 1)
        vecs, other_c, other_d, totals_a = barrier((vecs, other_c, other_d, totals_a))
        totals_c = dp_outward(pair_c, other_c)
        totals_d = dp_outward(pair_d, other_d)
        vecs = swap_sum(vecs, "dp", 4, 2)
    else:
        vecs = lax.psum(vecs, "dp")
        totals_a, totals_b, totals_c, totals_d = (
            (lax.psum(v.astype(F32), "dp"),) for v in (sum_a, sum_b, sum_c, sum_d)
        )

    def finish(totals, *at):
        return dp_finish(*[a[at] for a in totals])

    block_output = (
        block_input.astype(F32) + reduce_end(*mix_parts) + b_dense + b_out
    ).astype(BF16)
    d_input = d_out_f + reduce_end(*dx_parts)
    upper_rows = slice(0, half)
    lower_rows = slice(half, 2 * half)
    grad_w_in = jnp.concatenate(
        [finish(totals_a, upper_rows), finish(totals_b, upper_rows)], axis=1
    )
    grad_w_out = jnp.concatenate(
        [finish(totals_a, lower_rows), finish(totals_b, lower_rows)], axis=0
    )
    split = [finish(totals_c, slice(n * (inner + HEAD_DIM), (n + 1) * (inner + HEAD_DIM)))
             for n in range(heads - 1)] + [finish(totals_d, slice(0, inner + HEAD_DIM))]
    grad_w_qkv = jnp.concatenate([a[:inner] for a in split], axis=0).T
    grad_w_dense = jnp.concatenate([a[inner:] for a in split], axis=0)
    rest = vecs[: 5 * half].reshape(5, half)
    grad_b_in = vecs[5 * half : 5 * half + hid]
    grad_b_qkv = vecs[5 * half + hid :]
    return (
        block_output, d_input, grad_w_qkv, grad_b_qkv, grad_w_in, grad_b_in,
        grad_w_dense, rest[4], grad_w_out, rest[4], rest[0], rest[1], rest[2], rest[3],
    )


def solution(mesh):
    token = P(("dp", "col"), "row")
    placed = (
        token, P("row", "col"), P("col"), P("row", "col"), P("col"), P("col", "row"), P("row"),
        P("col", "row"), P("row"), P("row"), P("row"), P("row"), P("row"), P("dp"), P("dp"), token,
    )
    return jax.shard_map(
        local,
        mesh=mesh,
        in_specs=placed,
        out_specs=(
            token, token, P("row", "col"), P("col"), P("row", "col"), P("col"), P("col", "row"),
            P("row"), P("col", "row"), P("row"), P("row"), P("row"), P("row"), P("row"),
        ),
        check_vma=False,
    )
```

```python
import math

import jax
import jax.numpy as jnp
from jax import lax
from jax.experimental import pallas as pl
from jax.experimental.pallas import tpu as pltpu
from jax.sharding import PartitionSpec as P

D = 768
HEAD_DIM = 64
ROT = 16
SEQ_LEN = 1024
EPSILON = 1e-05
BLOCK = 256
F32 = jnp.float32
BF16 = jnp.bfloat16
GROUP = ("row", "col")
EXTRA = 16
VMEM_BYTES = 60 * 1024 * 1024


def dot_nn(a, b):
    return lax.dot_general(a, b, (((1,), (0,)), ((), ())), preferred_element_type=F32)


def dot_tn(a, b):
    return lax.dot_general(a, b, (((0,), (0,)), ((), ())), preferred_element_type=F32)


def dot_nt(a, b):
    return lax.dot_general(a, b, (((1,), (1,)), ((), ())), preferred_element_type=F32)


def normalize(x_rows):
    x = x_rows.astype(F32)
    mean = jnp.mean(x, axis=1, keepdims=True)
    centered = x - mean
    var = jnp.mean(centered * centered, axis=1, keepdims=True)
    inv_std = lax.rsqrt(var + EPSILON)
    return centered * inv_std, inv_std


def norm_back(grad, normed, inv_std):
    mean_grad = jnp.mean(grad, axis=1, keepdims=True)
    mean_cross = jnp.mean(grad * normed, axis=1, keepdims=True)
    return inv_std * (grad - mean_grad - normed * mean_cross)


def mlp_part(x_rows, go, wi_o, wi_p, wo_o, wo_p, b_ref, gain_ref, bias_ref, own_ref, send_acc):
    half = wi_o.shape[0]
    normed, _ = normalize(x_rows)
    h = (normed * gain_ref[...] + bias_ref[...]).astype(BF16)
    pre = dot_nn(h[:, :half], wi_o[...]) + dot_nn(h[:, half:], wi_p[...]) + b_ref[...]
    cdf = 0.5 * (1.0 + lax.erf(pre * (2.0 ** -0.5)))
    hidden = (pre * cdf).astype(BF16)
    slope = cdf + pre * (jnp.exp(-0.5 * pre * pre) * (1.0 / math.sqrt(2.0 * math.pi)))
    grad_hidden = dot_nt(go[:, :half], wo_o[...]) + dot_nt(go[:, half:], wo_p[...])
    grad_pre = (grad_hidden * slope).astype(BF16)
    own_ref[:half, :] += dot_tn(h[:, :half], grad_pre)
    send_acc[:half, :] += dot_tn(h[:, half:], grad_pre)
    own_ref[half:, :] += dot_tn(hidden, go[:, :half])
    send_acc[half:, :] += dot_tn(hidden, go[:, half:])
    return normed, hidden, grad_pre, jnp.sum(grad_pre.astype(F32), axis=0, keepdims=True)


def mlp_first_kernel(
    core_ref, xm_ref, xo_ref, gm_ref, go_ref, wi_o, wo_o, wi_p, wo_p, b_ref, gain_ref, bias_ref,
    again_ref, abias_ref,
    hid_ref, dp_ref, x_out, go_out, h_out, own_ref, send_ref,
    own_acc, acc_ref, sums,
):
    step = pl.program_id(0)

    @pl.when(step == 0)
    def _():
        own_acc[...] = jnp.zeros_like(own_acc)
        acc_ref[...] = jnp.zeros_like(acc_ref)
        sums[...] = jnp.zeros_like(sums)

    held = step // (pl.num_programs(0) // 2) == core_ref[0]
    x_rows = jnp.where(held, xm_ref[...], xo_ref[...])
    go = jnp.where(held, gm_ref[...], go_ref[...])
    x_out[...] = x_rows
    go_out[...] = go
    normed, hidden, grad_pre, gb = mlp_part(
        x_rows, go, wi_o, wi_p, wo_o, wo_p, b_ref, gain_ref, bias_ref, own_acc, acc_ref
    )
    h_out[...] = (normed * again_ref[...] + abias_ref[...]).astype(BF16)
    hid_ref[...] = hidden
    dp_ref[...] = grad_pre
    sums[0:1, :] += gb
    sums[EXTRA : EXTRA + 1, :] += gb
    total = jnp.sum(go.astype(F32), axis=0, keepdims=True)
    half = wi_o.shape[0]
    sums[1:2, :] += total[:, :half]
    sums[EXTRA + 1 : EXTRA + 2, :] += total[:, half:]

    @pl.when(step == pl.num_programs(0) - 1)
    def _():
        deep = own_acc.shape[0]
        own_ref[:deep, :] = own_acc[...].astype(BF16)
        send_ref[:deep, :] = acc_ref[...].astype(BF16)
        own_ref[deep:, :] = sums[:EXTRA, :].astype(BF16)
        send_ref[deep:, :] = sums[EXTRA:, :].astype(BF16)


def mlp_second_kernel(
    x_ref, go_ref, wi_o, wo_o, wi_p, wo_p, b_ref, gain_ref, bias_ref,
    hid_ref, dp_ref, own_ref, send_ref,
    own_acc, acc_ref, sums,
):
    step = pl.program_id(0)

    @pl.when(step == 0)
    def _():
        own_acc[...] = jnp.zeros_like(own_acc)
        acc_ref[...] = jnp.zeros_like(acc_ref)
        sums[...] = jnp.zeros_like(sums)

    _, hidden, grad_pre, gb = mlp_part(
        x_ref[...], go_ref[...], wi_o, wi_p, wo_o, wo_p, b_ref, gain_ref, bias_ref, own_acc, acc_ref
    )
    hid_ref[...] = hidden
    dp_ref[...] = grad_pre
    sums[0:1, :] += gb
    sums[EXTRA : EXTRA + 1, :] += gb

    @pl.when(step == pl.num_programs(0) - 1)
    def _():
        deep = own_acc.shape[0]
        own_ref[:deep, :] = own_acc[...].astype(BF16)
        send_ref[:deep, :] = acc_ref[...].astype(BF16)
        own_ref[deep:, :] = sums[:EXTRA, :].astype(BF16)
        send_ref[deep:, :] = sums[EXTRA:, :].astype(BF16)


def brief():
    return pl.CostEstimate(flops=1024, transcendentals=0, bytes_accessed=1024)


def whole(a):
    return pl.BlockSpec(a.shape, lambda *i: (0,) * a.ndim)


def shape(s, d):
    return jax.ShapeDtypeStruct(s, d)


def mlp_params():
    return pltpu.CompilerParams(
        dimension_semantics=("arbitrary",), vmem_limit_bytes=VMEM_BYTES
    )


def part_spec(size, at):
    return pl.BlockSpec((size, size), lambda *i: at)


def mlp_first(core, x_mine, x_other, go_mine, go_other, w_in, w_out, pack, b_in, *norms):
    held, width = x_mine.shape
    rows = 2 * held
    half = width // 2
    steps = held // BLOCK

    def held_map(i, core_ref):
        return (jnp.clip(i - core_ref[0] * steps, 0, steps - 1), 0)

    def other_map(i, core_ref):
        return (jnp.clip(i - (1 - core_ref[0]) * steps, 0, steps - 1), 0)

    mine_spec = pl.BlockSpec((BLOCK, width), held_map)
    other_spec = pl.BlockSpec((BLOCK, width), other_map)
    row_spec = pl.BlockSpec((BLOCK, width), lambda i, core_ref: (i, 0))
    half_spec = pl.BlockSpec((BLOCK, half), lambda i, core_ref: (i, 0))
    outs = [
        shape((rows, half), BF16),
        shape((rows, half), BF16),
        shape((rows, width), BF16),
        shape((rows, width), BF16),
        shape((rows, width), BF16),
        shape((2 * half + EXTRA, half), BF16),
        shape((2 * half + EXTRA, half), BF16),
    ]
    return pl.pallas_call(
        mlp_first_kernel,
        grid_spec=pltpu.PrefetchScalarGridSpec(
            num_scalar_prefetch=1,
            grid=(rows // BLOCK,),
            in_specs=[mine_spec, other_spec, mine_spec, other_spec]
            + [part_spec(half, (0, 0)), part_spec(half, (0, 0))]
            + [part_spec(half, (0, 0)), part_spec(half, (1, 0))]
            + [pl.BlockSpec((1, half), lambda *i: (0, 0))]
            + [whole(a) for a in norms],
            out_specs=[half_spec] * 2 + [row_spec] * 3 + [whole(a) for a in outs[5:]],
            scratch_shapes=[pltpu.VMEM((2 * half, half), F32)] * 2
            + [pltpu.VMEM((2 * EXTRA, half), F32)],
        ),
        out_shape=outs,
        compiler_params=mlp_params(),
        cost_estimate=brief(),
        name="mlp_first",
    )(core, x_mine, x_other, go_mine, go_other, w_in, w_out, pack, pack, b_in, *norms)


def mlp_second(x_seq, go_seq, w_in, w_out, pack, b_in, *norms):
    rows, width = x_seq.shape
    half = width // 2
    row_spec = pl.BlockSpec((BLOCK, width), lambda i: (i, 0))
    half_spec = pl.BlockSpec((BLOCK, half), lambda i: (i, 0))
    outs = [
        shape((rows, half), BF16),
        shape((rows, half), BF16),
        shape((2 * half + EXTRA, half), BF16),
        shape((2 * half + EXTRA, half), BF16),
    ]
    return pl.pallas_call(
        mlp_second_kernel,
        grid=(rows // BLOCK,),
        in_specs=[row_spec] * 2
        + [part_spec(half, (0, 1)), part_spec(half, (1, 0))]
        + [part_spec(half, (0, 0)), part_spec(half, (1, 0))]
        + [pl.BlockSpec((1, half), lambda *i: (0, 1))]
        + [whole(a) for a in norms],
        out_specs=[half_spec] * 2 + [whole(a) for a in outs[2:]],
        out_shape=outs,
        scratch_shapes=[pltpu.VMEM((2 * half, half), F32)] * 2
            + [pltpu.VMEM((2 * EXTRA, half), F32)],
        compiler_params=mlp_params(),
        cost_estimate=brief(),
        name="mlp_second",
    )(x_seq, go_seq, w_in, w_out, pack, pack, b_in, *norms)


def attn_kernel(
    h_ref, go_ref, wo_ref, wp_ref, b_ref, do_ref, dp_ref, cos_ref, s1_ref, s2_ref,
    segc_ref, segr_ref,
    ctx_out, dj_out, own_ref, send_ref,
    qk_ref, v_ref, dctx_ref, ctxt_ref, dqt_ref, dk_ref, dv_ref,
):
    rows = h_ref.shape[0]
    inner, half = wo_ref.shape
    tiles = rows // BLOCK
    lanes = lax.broadcasted_iota(jnp.int32, (1, 2 * HEAD_DIM), 1)
    scale = jnp.where(lanes < HEAD_DIM, HEAD_DIM ** (-0.5), 1.0)

    for t in range(tiles):
        at = slice(t * BLOCK, (t + 1) * BLOCK)
        joined = (
            dot_nt(h_ref[at, :half], wo_ref[...]) + dot_nt(h_ref[at, half:], wp_ref[...]) + b_ref[0]
        )
        u = joined[:, : 2 * HEAD_DIM]
        turned = (
            u * cos_ref[at, :]
            + pltpu.roll(u, 2 * HEAD_DIM - ROT // 2, 1) * s1_ref[at, :]
            + pltpu.roll(u, ROT // 2, 1) * s2_ref[at, :]
        )
        qk_ref[at, :] = (turned * scale).astype(BF16)
        v_ref[at, :] = joined[:, 2 * HEAD_DIM :].astype(BF16)
        dctx_ref[at, :] = (
            dot_nt(go_ref[at, :half], do_ref[...]) + dot_nt(go_ref[at, half:], dp_ref[...])
        ).astype(BF16)

    k_all = qk_ref[:, HEAD_DIM:]
    kt = k_all.astype(F32).T.astype(BF16)
    vt = v_ref[...].astype(F32).T.astype(BF16)
    for i in range(tiles):
        lo = i * BLOCK
        hi = lo + BLOCK
        q_blk = qk_ref[lo:hi, :HEAD_DIM]
        g_blk = dctx_ref[lo:hi, :]
        st = dot_nt(k_all[:hi], q_blk)
        key_at = lax.broadcasted_iota(jnp.int32, (hi, BLOCK), 0)
        query_at = lax.broadcasted_iota(jnp.int32, (hi, BLOCK), 1) + lo
        allowed = (segc_ref[0:hi, :] == segr_ref[:, lo:hi]) & (key_at <= query_at)
        st = jnp.where(allowed, st, -1e30)
        top = jnp.max(st, axis=0, keepdims=True)
        p = jnp.exp(st - top)
        p = p * (1.0 / jnp.sum(p, axis=0, keepdims=True))
        pb = p.astype(BF16)
        ctxt_ref[:, lo:hi] = dot_nn(vt[:, :hi], pb).astype(BF16)
        dpt = dot_nt(v_ref[0:hi, :], g_blk)
        inner_term = jnp.sum(dpt * p, axis=0, keepdims=True)
        dst = (p * (dpt - inner_term)).astype(BF16)
        dqt_ref[:, lo:hi] = dot_nn(kt[:, :hi], dst)
        dk_new = dot_nn(dst, q_blk)
        dv_new = dot_nn(pb, g_blk)
        if i > 0:
            dk_ref[0:lo, :] += dk_new[:lo]
            dv_ref[0:lo, :] += dv_new[:lo]
        dk_ref[lo:hi, :] = dk_new[lo:]
        dv_ref[lo:hi, :] = dv_new[lo:]

    ctx_out[0] = ctxt_ref[...]
    dq = dqt_ref[...].T
    back = jnp.concatenate([dq * HEAD_DIM ** (-0.5), dk_ref[...]], axis=1)
    turned_back = (
        back * cos_ref[...]
        + pltpu.roll(back * s2_ref[...], 2 * HEAD_DIM - ROT // 2, 1)
        + pltpu.roll(back * s1_ref[...], ROT // 2, 1)
    )
    dj = jnp.concatenate([turned_back.astype(BF16), dv_ref[...].astype(BF16)], axis=1)
    dj_out[0] = dj
    gb = jnp.sum(dj.astype(F32), axis=0, keepdims=True)
    gb = jnp.concatenate([gb, jnp.zeros((1, half - inner), F32)], axis=1)
    gb = jnp.concatenate([gb, jnp.zeros((EXTRA - 1, half), F32)], axis=0).astype(BF16)
    deep = inner + HEAD_DIM
    for out, at in ((own_ref, slice(0, half)), (send_ref, slice(half, 2 * half))):
        out[0, :inner, :] = dot_tn(dj, h_ref[:, at]).astype(BF16)
        out[0, inner:deep, :] = dot_nn(ctxt_ref[...], go_ref[:, at]).astype(BF16)
        out[0, deep:, :] = gb


def attn_head(first, count, h_seq, go_seq, wq_o, wq_p, b_heads, wd_o, wd_p, *tables):
    rows = h_seq.shape[0]
    half = wq_o.shape[1]
    inner = 3 * HEAD_DIM
    before = 2 * half
    deep = (before + wq_o.shape[0]) // HEAD_DIM
    before = before // inner

    def per_head(a, base):
        return pl.BlockSpec((1,) + a.shape[1:], lambda i: (i + base,) + (0,) * (a.ndim - 1))

    outs = [
        shape((count, HEAD_DIM, rows), BF16),
        shape((count, rows, inner), BF16),
        shape((count, inner + HEAD_DIM + EXTRA, half), BF16),
        shape((count, inner + HEAD_DIM + EXTRA, half), BF16),
    ]
    args = (h_seq, go_seq, wq_o, wq_p, b_heads, wd_o, wd_p) + tables
    specs = [whole(a) for a in args]
    specs[2] = pl.BlockSpec((inner, half), lambda i: (i + first, 0))
    specs[3] = pl.BlockSpec((inner, half), lambda i: (i + first + before, 0))
    specs[4] = per_head(b_heads, first)
    specs[5] = pl.BlockSpec((HEAD_DIM, half), lambda i: (i + first, 0))
    specs[6] = pl.BlockSpec((HEAD_DIM, half), lambda i: (i + first + deep, 0))
    return pl.pallas_call(
        attn_kernel,
        grid=(count,),
        in_specs=specs,
        out_specs=[per_head(a, 0) for a in outs],
        out_shape=outs,
        scratch_shapes=[
            pltpu.VMEM((rows, 2 * HEAD_DIM), BF16),
            pltpu.VMEM((rows, HEAD_DIM), BF16),
            pltpu.VMEM((rows, HEAD_DIM), BF16),
            pltpu.VMEM((HEAD_DIM, rows), BF16),
            pltpu.VMEM((HEAD_DIM, rows), F32),
            pltpu.VMEM((rows, HEAD_DIM), F32),
            pltpu.VMEM((rows, HEAD_DIM), F32),
        ],
        compiler_params=pltpu.CompilerParams(
            dimension_semantics=("arbitrary",), vmem_limit_bytes=VMEM_BYTES
        ),
        cost_estimate=brief(),
        name="attn_head",
    )(*args)


def close_kernel(
    core_ref, x_ref, hid_a, hid_b, dp_a, dp_b, c01, c2, j01, j2,
    wq_o, wd_o, wi_o, wo_o, got_a, got_b, again_ref, mgain_ref,
    mix_send, mix_keep, dx_send, dx_keep,
    vec_ref,
):
    del core_ref
    step = pl.program_id(0)
    sending = step < pl.num_programs(0) // 2
    half = wi_o.shape[0]
    inner = 3 * HEAD_DIM
    at_q = 2 * half
    at_d = at_q + wq_o.shape[0]

    @pl.when(step == 0)
    def _():
        vec_ref[...] = jnp.zeros_like(vec_ref)

    ctxt = jnp.concatenate([c01[0], c01[1], c2[0]], axis=0)
    mix = jnp.concatenate(
        [
            dot_tn(ctxt, wd_o[...])
            + dot_nn(hid_a[...], wo_o[:half, :]) + dot_nn(hid_b[...], wo_o[half:, :]),
            dot_tn(ctxt, got_b[at_d:, :])
            + dot_nn(hid_a[...], got_a[half:, :]) + dot_nn(hid_b[...], got_b[half:at_q, :]),
        ],
        axis=1,
    )
    grad_h = jnp.concatenate(
        [
            sum(
                dot_nn(j, w[at + n * inner : at + (n + 1) * inner, :])
                for n, j in enumerate((j01[0], j01[1], j2[0]))
            )
            for w, at in ((wq_o, 0), (got_b, at_q))
        ],
        axis=1,
    )
    grad_m = jnp.concatenate(
        [
            dot_nt(dp_a[...], wi_o[:, :half]) + dot_nt(dp_b[...], wi_o[:, half:]),
            dot_nt(dp_a[...], got_a[:half, :]) + dot_nt(dp_b[...], got_b[:half, :]),
        ],
        axis=1,
    )
    normed, inv_std = normalize(x_ref[...])
    vec_ref[0:1, :] += jnp.sum(grad_h * normed, axis=0, keepdims=True)
    vec_ref[1:2, :] += jnp.sum(grad_h, axis=0, keepdims=True)
    vec_ref[2:3, :] += jnp.sum(grad_m * normed, axis=0, keepdims=True)
    vec_ref[3:4, :] += jnp.sum(grad_m, axis=0, keepdims=True)
    dx = norm_back(grad_h * again_ref[...] + grad_m * mgain_ref[...], normed, inv_std)

    @pl.when(sending)
    def _():
        mix_send[...] = mix.astype(BF16)
        dx_send[pl.ds(step * BLOCK, BLOCK), :] = dx.astype(BF16)

    @pl.when(jnp.logical_not(sending))
    def _():
        mix_keep[...] = mix.astype(BF16)
        dx_keep[pl.ds((step - pl.num_programs(0) // 2) * BLOCK, BLOCK), :] = dx.astype(BF16)

    @pl.when(step == pl.num_programs(0) - 1)
    def _():
        held = dx_send.shape[0] - EXTRA
        dx_send[held:, :] = vec_ref[...].astype(BF16)
        dx_keep[held:, :] = vec_ref[...].astype(BF16)


def close_layer(core, x_seq, hidden, ctx, djs, *weights):
    rows, width = x_seq.shape
    held = rows // 2
    steps = held // BLOCK

    def block_of(i, core_ref):
        return jnp.where(i < steps, (1 - core_ref[0]) * steps + i, (core_ref[0] - 1) * steps + i)

    row_spec = pl.BlockSpec((BLOCK, width), lambda i, c: (block_of(i, c), 0))
    half_spec = pl.BlockSpec((BLOCK, width // 2), lambda i, c: (block_of(i, c), 0))
    send_spec = pl.BlockSpec((BLOCK, width), lambda i, c: (jnp.minimum(i, steps - 1), 0))
    keep_spec = pl.BlockSpec((BLOCK, width), lambda i, c: (jnp.maximum(i - steps, 0), 0))
    ctx_specs = [
        pl.BlockSpec((a.shape[0], HEAD_DIM, BLOCK), lambda i, c: (0, 0, block_of(i, c)))
        for a in ctx
    ]
    dj_specs = [
        pl.BlockSpec((a.shape[0], BLOCK, 3 * HEAD_DIM), lambda i, c: (0, block_of(i, c), 0))
        for a in djs
    ]
    outs = [shape((held, width), BF16)] * 2 + [shape((held + EXTRA, width), BF16)] * 2
    return pl.pallas_call(
        close_kernel,
        grid_spec=pltpu.PrefetchScalarGridSpec(
            num_scalar_prefetch=1,
            grid=(rows // BLOCK,),
            in_specs=[row_spec] + [half_spec] * 4 + ctx_specs + dj_specs
            + [whole(a) for a in weights],
            out_specs=[send_spec, keep_spec, whole(outs[2]), whole(outs[3])],
            scratch_shapes=[pltpu.VMEM((EXTRA, width), F32)],
        ),
        out_shape=outs,
        compiler_params=pltpu.CompilerParams(
            dimension_semantics=("arbitrary",), vmem_limit_bytes=VMEM_BYTES
        ),
        cost_estimate=brief(),
        name="close_layer",
    )(core, x_seq, *hidden, *ctx, *djs, *weights)


def group_perm(n_row, n_col, target):
    pairs = []
    for r in range(n_row):
        for c in range(n_col):
            to = target(r, c // 2, c % 2)
            if to is not None:
                pairs.append((r * n_col + c, to[0] * n_col + 2 * to[1] + to[2]))
    return pairs


def swap_row(value):
    return lax.ppermute(value, "row", [(0, 1), (1, 0)])


def dp_inward(value):
    return lax.ppermute(value, "dp", [(0, 1), (3, 2)])


def dp_middle(value, inward):
    pair = (value.astype(F32) + inward.astype(F32)).astype(BF16)
    return pair, lax.ppermute(pair, "dp", [(1, 2), (2, 1)])


def dp_outward(pair, other):
    total = (pair.astype(F32) + other.astype(F32)).astype(BF16)
    return total, lax.ppermute(total, "dp", [(1, 0), (2, 3)])


def dp_finish(total, outward=None):
    if outward is None:
        return total
    place = lax.axis_index("dp")
    return jnp.where((place == 1) | (place == 2), total, outward).astype(F32)


def swap_sum(value, axis, size, bit):
    return value + lax.ppermute(value, axis, [(i, i ^ bit) for i in range(size)])


def local(
    block_input, w_qkv, b_qkv, w_in, b_in, w_dense, b_dense, w_out, b_out,
    ln_attn_gain, ln_attn_bias, ln_mlp_gain, ln_mlp_bias, segments, positions, d_out,
):
    n_row = lax.axis_size("row")
    n_col = lax.axis_size("col")
    n_dp = lax.axis_size("dp")
    row = lax.axis_index("row")
    col = lax.axis_index("col")
    half = block_input.shape[1]
    barrier = lax.optimization_barrier
    upper = col // 2
    core = col % 2
    home = row == upper
    heads = w_qkv.shape[1] // (3 * HEAD_DIM)

    spread = group_perm(
        n_row, n_col, lambda r, u, k: (r, 1 - u, k) if r == u else (1 - r, u, k)
    )
    cross = group_perm(n_row, n_col, lambda r, u, k: None if r == u else (1 - r, 1 - u, k))
    pair = group_perm(n_row, n_col, lambda r, u, k: (r, u, 1 - k))
    forward = group_perm(n_row, n_col, lambda r, u, k: (r, 1 - u, k) if r == u else None)
    collect = group_perm(
        n_row, n_col, lambda r, u, k: (1 - r, u, k) if r == u else (r, 1 - u, k)
    )

    chain = n_dp == 4
    inner = 3 * HEAD_DIM
    wq_t = w_qkv.T
    pack_a = jnp.concatenate([w_in[:, :half], w_out[:half]], axis=0)
    pack_b = jnp.concatenate([w_in[:, half:], w_out[half:], wq_t, w_dense], axis=0)
    norms = jnp.stack([ln_attn_gain, ln_attn_bias, ln_mlp_gain, ln_mlp_bias])
    core_at = core.reshape(1)

    at_seq = row * SEQ_LEN
    seg_seq = lax.dynamic_slice_in_dim(segments, at_seq, SEQ_LEN)
    pos_seq = lax.dynamic_slice_in_dim(positions, at_seq, SEQ_LEN)
    lane = jnp.arange(2 * HEAD_DIM) % HEAD_DIM
    freq_steps = (lane % (ROT // 2)).astype(F32) * (-2.0 * math.log(10000.0) / ROT)
    freq = jnp.where(lane < ROT, jnp.exp(freq_steps), 0.0)
    angles = pos_seq.astype(F32)[:, None] * freq[None, :]
    cos_table = jnp.cos(angles)
    sin_table = jnp.sin(angles)
    sin_up = jnp.where(lane < ROT // 2, -sin_table, 0.0)
    sin_down = jnp.where((lane >= ROT // 2) & (lane < ROT), sin_table, 0.0)

    def join(block, near, far):
        return jnp.concatenate(
            [jnp.where(home, block, near), jnp.where(home, near, far)], axis=1
        )

    d_out_f = d_out.astype(F32)
    norms_got = swap_row(norms)
    near_x = lax.ppermute(block_input, GROUP, spread)
    segc = seg_seq[:, None]
    go_in, cos_table, sin_up, sin_down, pack_a, pack_b, segc = barrier(
        (d_out, cos_table, sin_up, sin_down, pack_a, pack_b, segc)
    )
    near_go = lax.ppermute(go_in, GROUP, spread)
    near_x, norms, norms_got, pack_a = barrier((near_x, norms, norms_got, pack_a))
    far_x = lax.ppermute(near_x, GROUP, forward)
    got_a = swap_row(pack_a)
    far_go = lax.ppermute(near_go, GROUP, forward)
    x_mine = join(block_input, near_x, far_x)
    x_other = lax.ppermute(x_mine, GROUP, pair)
    far_go, got_a = barrier((far_go, got_a))
    go_mine = join(d_out, near_go, far_go)
    go_other = lax.ppermute(go_mine, GROUP, pair)
    got_b = swap_row(pack_b)
    norms = jnp.concatenate([norms, norms_got], axis=1)

    hid_a, dp_a, x_seq, go_seq, h_seq, own_a, send_a = mlp_first(
        core_at, x_mine, x_other, go_mine, go_other, w_in, w_out, got_a, b_in[None],
        norms[2:3], norms[3:4], norms[0:1], norms[1:2],
    )
    x_seq, send_a = barrier((x_seq, send_a))
    back_a = swap_row(send_a)
    hid_b, dp_b, own_b, send_b = mlp_second(
        x_seq, go_seq, w_in, w_out, got_b, b_in[None], norms[2:3], norms[3:4]
    )
    h_seq, send_b = barrier((h_seq, send_b))
    back_b = swap_row(send_b)
    width = wq_t.shape[0]
    heads_args = (
        wq_t, got_b, b_qkv.reshape(heads, 1, inner), w_dense, got_b,
        cos_table, sin_up, sin_down, segc, seg_seq[None, :],
    )

    def payload_sum(own, got):
        return (own.astype(F32) + got.astype(F32)).astype(BF16)

    heads01 = attn_head(0, heads - 1, h_seq, go_seq, *heads_args)
    go_seq, heads01, back_a, back_b = barrier((go_seq, heads01, back_a, back_b))
    back01 = swap_row(heads01[3])
    sum_a = payload_sum(own_a, back_a)
    sum_b = payload_sum(own_b, back_b)
    if chain:
        in_a = dp_inward(sum_a)
        in_b = dp_inward(sum_b)
    head2 = attn_head(heads - 1, 1, h_seq, go_seq, *heads_args)
    x_seq, head2, back01 = barrier((x_seq, head2, back01))
    back2 = swap_row(head2[3])
    sum_c = payload_sum(heads01[2], back01).reshape(-1, half)
    if chain:
        x_seq, in_a, sum_a = barrier((x_seq, in_a, sum_a))
        pair_a, other_a = dp_middle(sum_a, in_a)
        in_c = dp_inward(sum_c)
    done = [heads01, head2]
    mix_s, mix_k, dx_s, dx_k = close_layer(
        core_at, x_seq, [hid_a, hid_b, dp_a, dp_b], [a[0] for a in done], [a[1] for a in done],
        wq_t, w_dense, w_in, w_out, got_a, got_b, norms[0:1], norms[2:3],
    )
    if chain:
        mix_s, dx_s, in_b, sum_b, in_c, sum_c, pair_a, other_a = barrier(
            (mix_s, dx_s, in_b, sum_b, in_c, sum_c, pair_a, other_a)
        )
        totals_a = dp_outward(pair_a, other_a)
        pair_b, other_b = dp_middle(sum_b, in_b)
        pair_c, other_c = dp_middle(sum_c, in_c)
    mix_got = lax.ppermute(mix_s, GROUP, pair)
    dx_got = lax.ppermute(dx_s, GROUP, pair)
    mix_got, dx_got, back2 = barrier((mix_got, dx_got, back2))
    sum_d = payload_sum(head2[2], back2).reshape(-1, half)
    if chain:
        in_d = dp_inward(sum_d)

    def reduce_start(got, kept):
        low_sum = (kept.astype(F32) + got.astype(F32)).astype(BF16)
        near = lax.ppermute(
            jnp.where(home, low_sum[:, half:], low_sum[:, :half]), GROUP, collect
        )
        return near, lax.ppermute(low_sum[:, half:], GROUP, cross), low_sum[:, :half]

    def reduce_end(near, far, kept):
        return near.astype(F32) + jnp.where(home, kept, far).astype(F32)

    held = block_input.shape[0]
    norm_sums = dx_k[held : held + 4].astype(F32) + dx_got[held : held + 4].astype(F32)
    rest = norm_sums[:, :half] + swap_row(norm_sums[:, half:])
    rest = swap_sum(rest, "col", n_col, 2)
    mix_got, dx_got, rest = barrier((mix_got, dx_got, rest))
    mix_parts = reduce_start(mix_got, mix_k)
    dx_parts = reduce_start(dx_got[:held], dx_k[:held])
    if chain:
        rest = swap_sum(rest, "dp", 4, 1)
    if chain:
        in_d, sum_d, pair_b, other_b = barrier((in_d, sum_d, pair_b, other_b))
        totals_b = dp_outward(pair_b, other_b)
        pair_d, other_d = dp_middle(sum_d, in_d)
        mix_parts, dx_parts, pair_c, other_c, totals_a, rest = barrier(
            (mix_parts, dx_parts, pair_c, other_c, totals_a, rest)
        )
        rest = swap_sum(rest, "dp", 4, 2)
        totals_c = dp_outward(pair_c, other_c)
        totals_d = dp_outward(pair_d, other_d)
    dx_total = reduce_end(*dx_parts)
    if not chain:
        rest = lax.psum(rest, "dp")
        totals_a, totals_b, totals_c, totals_d = (
            (lax.psum(v.astype(F32), "dp"),) for v in (sum_a, sum_b, sum_c, sum_d)
        )

    def finish(totals, *at):
        return dp_finish(*[a[at] for a in totals])

    block_output = (
        block_input.astype(F32) + reduce_end(*mix_parts) + b_dense + b_out
    ).astype(BF16)
    d_input = d_out_f + dx_total
    upper_rows = slice(0, half)
    lower_rows = slice(half, 2 * half)
    grad_w_in = jnp.concatenate(
        [finish(totals_a, upper_rows), finish(totals_b, upper_rows)], axis=1
    )
    grad_w_out = jnp.concatenate(
        [finish(totals_a, lower_rows), finish(totals_b, lower_rows)], axis=0
    )
    deep = inner + HEAD_DIM
    step = deep + EXTRA
    split = [finish(totals_c, slice(n * step, n * step + step)) for n in range(heads - 1)]
    split = split + [finish(totals_d, slice(0, step))]
    grad_w_qkv = jnp.concatenate([a[:inner] for a in split], axis=0).T
    grad_w_dense = jnp.concatenate([a[inner:deep] for a in split], axis=0)
    grad_b_qkv = jnp.concatenate([a[deep, :inner] for a in split])
    grad_b_in = jnp.concatenate(
        [finish(totals_a, 2 * half), finish(totals_b, 2 * half)]
    )
    grad_b_out = finish(totals_a, 2 * half + 1)
    return (
        block_output, d_input, grad_w_qkv, grad_b_qkv, grad_w_in, grad_b_in,
        grad_w_dense, grad_b_out, grad_w_out, grad_b_out, rest[0], rest[1], rest[2], rest[3],
    )


def solution(mesh):
    token = P(("dp", "col"), "row")
    placed = (
        token, P("row", "col"), P("col"), P("row", "col"), P("col"), P("col", "row"), P("row"),
        P("col", "row"), P("row"), P("row"), P("row"), P("row"), P("row"), P("dp"), P("dp"), token,
    )
    return jax.shard_map(
        local,
        mesh=mesh,
        in_specs=placed,
        out_specs=(
            token, token, P("row", "col"), P("col"), P("row", "col"), P("col"), P("col", "row"),
            P("row"), P("col", "row"), P("row"), P("row"), P("row"), P("row"), P("row"),
        ),
        check_vma=False,
    )
```

```python
import math

import jax
import jax.numpy as jnp
from jax import lax
from jax.experimental import pallas as pl
from jax.experimental.pallas import tpu as pltpu
from jax.sharding import PartitionSpec as P

D = 768
HEAD_DIM = 64
ROT = 16
SEQ_LEN = 1024
EPSILON = 1e-05
BLOCK = 256
F32 = jnp.float32
BF16 = jnp.bfloat16
GROUP = ("row", "col")
EXTRA = 16
VMEM_BYTES = 60 * 1024 * 1024


def dot_nn(a, b):
    return lax.dot_general(a, b, (((1,), (0,)), ((), ())), preferred_element_type=F32)


def dot_tn(a, b):
    return lax.dot_general(a, b, (((0,), (0,)), ((), ())), preferred_element_type=F32)


def dot_nt(a, b):
    return lax.dot_general(a, b, (((1,), (1,)), ((), ())), preferred_element_type=F32)


def normalize(x_rows):
    x = x_rows.astype(F32)
    mean = jnp.mean(x, axis=1, keepdims=True)
    centered = x - mean
    var = jnp.mean(centered * centered, axis=1, keepdims=True)
    inv_std = lax.rsqrt(var + EPSILON)
    return centered * inv_std, inv_std


def norm_back(grad, normed, inv_std):
    mean_grad = jnp.mean(grad, axis=1, keepdims=True)
    mean_cross = jnp.mean(grad * normed, axis=1, keepdims=True)
    return inv_std * (grad - mean_grad - normed * mean_cross)


def mlp_part(x_rows, go, wi_o, wi_p, wo_o, wo_p, b_ref, gain_ref, bias_ref, own_ref, send_acc):
    half = wi_o.shape[0]
    normed, _ = normalize(x_rows)
    h = (normed * gain_ref[...] + bias_ref[...]).astype(BF16)
    pre = dot_nn(h[:, :half], wi_o[...]) + dot_nn(h[:, half:], wi_p[...]) + b_ref[...]
    cdf = 0.5 * (1.0 + lax.erf(pre * (2.0 ** -0.5)))
    hidden = (pre * cdf).astype(BF16)
    slope = cdf + pre * (jnp.exp(-0.5 * pre * pre) * (1.0 / math.sqrt(2.0 * math.pi)))
    grad_hidden = dot_nt(go[:, :half], wo_o[...]) + dot_nt(go[:, half:], wo_p[...])
    grad_pre = (grad_hidden * slope).astype(BF16)
    own_ref[:half, :] += dot_tn(h[:, :half], grad_pre)
    send_acc[:half, :] += dot_tn(h[:, half:], grad_pre)
    own_ref[half:, :] += dot_tn(hidden, go[:, :half])
    send_acc[half:, :] += dot_tn(hidden, go[:, half:])
    return normed, hidden, grad_pre, jnp.sum(grad_pre.astype(F32), axis=0, keepdims=True)


def mlp_first_kernel(
    core_ref, xm_ref, xo_ref, gm_ref, go_ref, wi_o, wo_o, wi_p, wo_p, b_ref, gain_ref, bias_ref,
    again_ref, abias_ref,
    hid_ref, dp_ref, x_out, go_out, h_out, own_ref, send_ref,
    own_acc, acc_ref, sums,
):
    step = pl.program_id(0)

    @pl.when(step == 0)
    def _():
        own_acc[...] = jnp.zeros_like(own_acc)
        acc_ref[...] = jnp.zeros_like(acc_ref)
        sums[...] = jnp.zeros_like(sums)

    held = step // (pl.num_programs(0) // 2) == core_ref[0]
    x_rows = jnp.where(held, xm_ref[...], xo_ref[...])
    go = jnp.where(held, gm_ref[...], go_ref[...])
    x_out[...] = x_rows
    go_out[...] = go
    normed, hidden, grad_pre, gb = mlp_part(
        x_rows, go, wi_o, wi_p, wo_o, wo_p, b_ref, gain_ref, bias_ref, own_acc, acc_ref
    )
    h_out[...] = (normed * again_ref[...] + abias_ref[...]).astype(BF16)
    hid_ref[...] = hidden
    dp_ref[...] = grad_pre
    sums[0:1, :] += gb
    sums[EXTRA : EXTRA + 1, :] += gb
    total = jnp.sum(go.astype(F32), axis=0, keepdims=True)
    half = wi_o.shape[0]
    sums[1:2, :] += total[:, :half]
    sums[EXTRA + 1 : EXTRA + 2, :] += total[:, half:]

    @pl.when(step == pl.num_programs(0) - 1)
    def _():
        deep = own_acc.shape[0]
        own_ref[:deep, :] = own_acc[...].astype(BF16)
        send_ref[:deep, :] = acc_ref[...].astype(BF16)
        own_ref[deep:, :] = sums[:EXTRA, :].astype(BF16)
        send_ref[deep:, :] = sums[EXTRA:, :].astype(BF16)


def mlp_second_kernel(
    x_ref, go_ref, wi_o, wo_o, wi_p, wo_p, b_ref, gain_ref, bias_ref,
    hid_ref, dp_ref, own_ref, send_ref,
    own_acc, acc_ref, sums,
):
    step = pl.program_id(0)

    @pl.when(step == 0)
    def _():
        own_acc[...] = jnp.zeros_like(own_acc)
        acc_ref[...] = jnp.zeros_like(acc_ref)
        sums[...] = jnp.zeros_like(sums)

    _, hidden, grad_pre, gb = mlp_part(
        x_ref[...], go_ref[...], wi_o, wi_p, wo_o, wo_p, b_ref, gain_ref, bias_ref, own_acc, acc_ref
    )
    hid_ref[...] = hidden
    dp_ref[...] = grad_pre
    sums[0:1, :] += gb
    sums[EXTRA : EXTRA + 1, :] += gb

    @pl.when(step == pl.num_programs(0) - 1)
    def _():
        deep = own_acc.shape[0]
        own_ref[:deep, :] = own_acc[...].astype(BF16)
        send_ref[:deep, :] = acc_ref[...].astype(BF16)
        own_ref[deep:, :] = sums[:EXTRA, :].astype(BF16)
        send_ref[deep:, :] = sums[EXTRA:, :].astype(BF16)


def brief():
    return pl.CostEstimate(flops=1024, transcendentals=0, bytes_accessed=1024)


def whole(a):
    return pl.BlockSpec(a.shape, lambda *i: (0,) * a.ndim)


def shape(s, d):
    return jax.ShapeDtypeStruct(s, d)


def mlp_params():
    return pltpu.CompilerParams(
        dimension_semantics=("arbitrary",), vmem_limit_bytes=VMEM_BYTES
    )


def part_spec(size, at):
    return pl.BlockSpec((size, size), lambda *i: at)


def mlp_first(core, x_mine, x_other, go_mine, go_other, w_in, w_out, pack, b_in, *norms):
    held, width = x_mine.shape
    rows = 2 * held
    half = width // 2
    steps = held // BLOCK

    def held_map(i, core_ref):
        return (jnp.clip(i - core_ref[0] * steps, 0, steps - 1), 0)

    def other_map(i, core_ref):
        return (jnp.clip(i - (1 - core_ref[0]) * steps, 0, steps - 1), 0)

    mine_spec = pl.BlockSpec((BLOCK, width), held_map)
    other_spec = pl.BlockSpec((BLOCK, width), other_map)
    row_spec = pl.BlockSpec((BLOCK, width), lambda i, core_ref: (i, 0))
    half_spec = pl.BlockSpec((BLOCK, half), lambda i, core_ref: (i, 0))
    outs = [
        shape((rows, half), BF16),
        shape((rows, half), BF16),
        shape((rows, width), BF16),
        shape((rows, width), BF16),
        shape((rows, width), BF16),
        shape((2 * half + EXTRA, half), BF16),
        shape((2 * half + EXTRA, half), BF16),
    ]
    return pl.pallas_call(
        mlp_first_kernel,
        grid_spec=pltpu.PrefetchScalarGridSpec(
            num_scalar_prefetch=1,
            grid=(rows // BLOCK,),
            in_specs=[mine_spec, other_spec, mine_spec, other_spec]
            + [part_spec(half, (0, 0)), part_spec(half, (0, 0))]
            + [part_spec(half, (0, 0)), part_spec(half, (1, 0))]
            + [pl.BlockSpec((1, half), lambda *i: (0, 0))]
            + [whole(a) for a in norms],
            out_specs=[half_spec] * 2 + [row_spec] * 3 + [whole(a) for a in outs[5:]],
            scratch_shapes=[pltpu.VMEM((2 * half, half), F32)] * 2
            + [pltpu.VMEM((2 * EXTRA, half), F32)],
        ),
        out_shape=outs,
        compiler_params=mlp_params(),
        cost_estimate=brief(),
        name="mlp_first",
    )(core, x_mine, x_other, go_mine, go_other, w_in, w_out, pack, pack, b_in, *norms)


def mlp_second(x_seq, go_seq, w_in, w_out, pack, b_in, *norms):
    rows, width = x_seq.shape
    half = width // 2
    row_spec = pl.BlockSpec((BLOCK, width), lambda i: (i, 0))
    half_spec = pl.BlockSpec((BLOCK, half), lambda i: (i, 0))
    outs = [
        shape((rows, half), BF16),
        shape((rows, half), BF16),
        shape((2 * half + EXTRA, half), BF16),
        shape((2 * half + EXTRA, half), BF16),
    ]
    return pl.pallas_call(
        mlp_second_kernel,
        grid=(rows // BLOCK,),
        in_specs=[row_spec] * 2
        + [part_spec(half, (0, 1)), part_spec(half, (1, 0))]
        + [part_spec(half, (0, 0)), part_spec(half, (1, 0))]
        + [pl.BlockSpec((1, half), lambda *i: (0, 1))]
        + [whole(a) for a in norms],
        out_specs=[half_spec] * 2 + [whole(a) for a in outs[2:]],
        out_shape=outs,
        scratch_shapes=[pltpu.VMEM((2 * half, half), F32)] * 2
            + [pltpu.VMEM((2 * EXTRA, half), F32)],
        compiler_params=mlp_params(),
        cost_estimate=brief(),
        name="mlp_second",
    )(x_seq, go_seq, w_in, w_out, pack, pack, b_in, *norms)


def attn_kernel(
    h_ref, go_ref, wo_ref, wp_ref, b_ref, do_ref, dp_ref, cos_ref, s1_ref, s2_ref,
    segc_ref, segr_ref,
    ctx_out, dj_out, own_ref, send_ref,
    qk_ref, v_ref, dctx_ref, ctxt_ref, dqt_ref, dk_ref, dv_ref,
):
    rows = h_ref.shape[0]
    inner, half = wo_ref.shape
    tiles = rows // BLOCK
    lanes = lax.broadcasted_iota(jnp.int32, (1, 2 * HEAD_DIM), 1)
    scale = jnp.where(lanes < HEAD_DIM, HEAD_DIM ** (-0.5), 1.0)

    for t in range(tiles):
        at = slice(t * BLOCK, (t + 1) * BLOCK)
        joined = (
            dot_nt(h_ref[at, :half], wo_ref[...]) + dot_nt(h_ref[at, half:], wp_ref[...]) + b_ref[0]
        )
        u = joined[:, : 2 * HEAD_DIM]
        turned = (
            u * cos_ref[at, :]
            + pltpu.roll(u, 2 * HEAD_DIM - ROT // 2, 1) * s1_ref[at, :]
            + pltpu.roll(u, ROT // 2, 1) * s2_ref[at, :]
        )
        qk_ref[at, :] = (turned * scale).astype(BF16)
        v_ref[at, :] = joined[:, 2 * HEAD_DIM :].astype(BF16)
        dctx_ref[at, :] = (
            dot_nt(go_ref[at, :half], do_ref[...]) + dot_nt(go_ref[at, half:], dp_ref[...])
        ).astype(BF16)

    k_all = qk_ref[:, HEAD_DIM:]
    kt = k_all.astype(F32).T.astype(BF16)
    vt = v_ref[...].astype(F32).T.astype(BF16)
    for i in range(tiles):
        lo = i * BLOCK
        hi = lo + BLOCK
        q_blk = qk_ref[lo:hi, :HEAD_DIM]
        g_blk = dctx_ref[lo:hi, :]
        st = dot_nt(k_all[:hi], q_blk)
        key_at = lax.broadcasted_iota(jnp.int32, (hi, BLOCK), 0)
        query_at = lax.broadcasted_iota(jnp.int32, (hi, BLOCK), 1) + lo
        allowed = (segc_ref[0:hi, :] == segr_ref[:, lo:hi]) & (key_at <= query_at)
        st = jnp.where(allowed, st, -1e30)
        top = jnp.max(st, axis=0, keepdims=True)
        p = jnp.exp(st - top)
        p = p * (1.0 / jnp.sum(p, axis=0, keepdims=True))
        pb = p.astype(BF16)
        ctxt_ref[:, lo:hi] = dot_nn(vt[:, :hi], pb).astype(BF16)
        dpt = dot_nt(v_ref[0:hi, :], g_blk)
        inner_term = jnp.sum(dpt * p, axis=0, keepdims=True)
        dst = (p * (dpt - inner_term)).astype(BF16)
        dqt_ref[:, lo:hi] = dot_nn(kt[:, :hi], dst)
        dk_new = dot_nn(dst, q_blk)
        dv_new = dot_nn(pb, g_blk)
        if i > 0:
            dk_ref[0:lo, :] += dk_new[:lo]
            dv_ref[0:lo, :] += dv_new[:lo]
        dk_ref[lo:hi, :] = dk_new[lo:]
        dv_ref[lo:hi, :] = dv_new[lo:]

    ctx_out[0] = ctxt_ref[...]
    dq = dqt_ref[...].T
    back = jnp.concatenate([dq * HEAD_DIM ** (-0.5), dk_ref[...]], axis=1)
    turned_back = (
        back * cos_ref[...]
        + pltpu.roll(back * s2_ref[...], 2 * HEAD_DIM - ROT // 2, 1)
        + pltpu.roll(back * s1_ref[...], ROT // 2, 1)
    )
    dj = jnp.concatenate([turned_back.astype(BF16), dv_ref[...].astype(BF16)], axis=1)
    dj_out[0] = dj
    gb = jnp.sum(dj.astype(F32), axis=0, keepdims=True)
    gb = jnp.concatenate([gb, jnp.zeros((1, half - inner), F32)], axis=1)
    gb = jnp.concatenate([gb, jnp.zeros((EXTRA - 1, half), F32)], axis=0).astype(BF16)
    deep = inner + HEAD_DIM
    for out, at in ((own_ref, slice(0, half)), (send_ref, slice(half, 2 * half))):
        out[0, :inner, :] = dot_tn(dj, h_ref[:, at]).astype(BF16)
        out[0, inner:deep, :] = dot_nn(ctxt_ref[...], go_ref[:, at]).astype(BF16)
        out[0, deep:, :] = gb


def attn_head(first, count, h_seq, go_seq, wq_o, wq_p, b_heads, wd_o, wd_p, *tables):
    rows = h_seq.shape[0]
    half = wq_o.shape[1]
    inner = 3 * HEAD_DIM
    before = 2 * half
    deep = (before + wq_o.shape[0]) // HEAD_DIM
    before = before // inner

    def per_head(a, base):
        return pl.BlockSpec((1,) + a.shape[1:], lambda i: (i + base,) + (0,) * (a.ndim - 1))

    outs = [
        shape((count, HEAD_DIM, rows), BF16),
        shape((count, rows, inner), BF16),
        shape((count, inner + HEAD_DIM + EXTRA, half), BF16),
        shape((count, inner + HEAD_DIM + EXTRA, half), BF16),
    ]
    args = (h_seq, go_seq, wq_o, wq_p, b_heads, wd_o, wd_p) + tables
    specs = [whole(a) for a in args]
    specs[2] = pl.BlockSpec((inner, half), lambda i: (i + first, 0))
    specs[3] = pl.BlockSpec((inner, half), lambda i: (i + first + before, 0))
    specs[4] = per_head(b_heads, first)
    specs[5] = pl.BlockSpec((HEAD_DIM, half), lambda i: (i + first, 0))
    specs[6] = pl.BlockSpec((HEAD_DIM, half), lambda i: (i + first + deep, 0))
    return pl.pallas_call(
        attn_kernel,
        grid=(count,),
        in_specs=specs,
        out_specs=[per_head(a, 0) for a in outs],
        out_shape=outs,
        scratch_shapes=[
            pltpu.VMEM((rows, 2 * HEAD_DIM), BF16),
            pltpu.VMEM((rows, HEAD_DIM), BF16),
            pltpu.VMEM((rows, HEAD_DIM), BF16),
            pltpu.VMEM((HEAD_DIM, rows), BF16),
            pltpu.VMEM((HEAD_DIM, rows), F32),
            pltpu.VMEM((rows, HEAD_DIM), F32),
            pltpu.VMEM((rows, HEAD_DIM), F32),
        ],
        compiler_params=pltpu.CompilerParams(
            dimension_semantics=("arbitrary",), vmem_limit_bytes=VMEM_BYTES
        ),
        cost_estimate=brief(),
        name="attn_head",
    )(*args)


def close_kernel(
    core_ref, x_ref, hid_a, hid_b, dp_a, dp_b, c01, c2, j01, j2,
    wq_o, wd_o, wi_o, wo_o, got_a, got_b, again_ref, mgain_ref,
    mix_send, mix_keep, dx_send, dx_keep,
    vec_ref,
):
    del core_ref
    step = pl.program_id(0)
    sending = step < pl.num_programs(0) // 2
    half = wi_o.shape[0]
    inner = 3 * HEAD_DIM
    at_q = 2 * half
    at_d = at_q + wq_o.shape[0]

    @pl.when(step == 0)
    def _():
        vec_ref[...] = jnp.zeros_like(vec_ref)

    ctxt = jnp.concatenate([c01[0], c01[1], c2[0]], axis=0)
    mix = jnp.concatenate(
        [
            dot_tn(ctxt, wd_o[...])
            + dot_nn(hid_a[...], wo_o[:half, :]) + dot_nn(hid_b[...], wo_o[half:, :]),
            dot_tn(ctxt, got_b[at_d:, :])
            + dot_nn(hid_a[...], got_a[half:, :]) + dot_nn(hid_b[...], got_b[half:at_q, :]),
        ],
        axis=1,
    )
    grad_h = jnp.concatenate(
        [
            sum(
                dot_nn(j, w[at + n * inner : at + (n + 1) * inner, :])
                for n, j in enumerate((j01[0], j01[1], j2[0]))
            )
            for w, at in ((wq_o, 0), (got_b, at_q))
        ],
        axis=1,
    )
    grad_m = jnp.concatenate(
        [
            dot_nt(dp_a[...], wi_o[:, :half]) + dot_nt(dp_b[...], wi_o[:, half:]),
            dot_nt(dp_a[...], got_a[:half, :]) + dot_nt(dp_b[...], got_b[:half, :]),
        ],
        axis=1,
    )
    normed, inv_std = normalize(x_ref[...])
    vec_ref[0:1, :] += jnp.sum(grad_h * normed, axis=0, keepdims=True)
    vec_ref[1:2, :] += jnp.sum(grad_h, axis=0, keepdims=True)
    vec_ref[2:3, :] += jnp.sum(grad_m * normed, axis=0, keepdims=True)
    vec_ref[3:4, :] += jnp.sum(grad_m, axis=0, keepdims=True)
    dx = norm_back(grad_h * again_ref[...] + grad_m * mgain_ref[...], normed, inv_std)

    @pl.when(sending)
    def _():
        mix_send[...] = mix.astype(BF16)
        dx_send[pl.ds(step * BLOCK, BLOCK), :] = dx.astype(BF16)

    @pl.when(jnp.logical_not(sending))
    def _():
        mix_keep[...] = mix.astype(BF16)
        dx_keep[pl.ds((step - pl.num_programs(0) // 2) * BLOCK, BLOCK), :] = dx.astype(BF16)

    @pl.when(step == pl.num_programs(0) - 1)
    def _():
        held = dx_send.shape[0] - EXTRA
        dx_send[held:, :] = vec_ref[...].astype(BF16)
        dx_keep[held:, :] = vec_ref[...].astype(BF16)


def close_layer(core, x_seq, hidden, ctx, djs, *weights):
    rows, width = x_seq.shape
    held = rows // 2
    steps = held // BLOCK

    def block_of(i, core_ref):
        return jnp.where(i < steps, (1 - core_ref[0]) * steps + i, (core_ref[0] - 1) * steps + i)

    row_spec = pl.BlockSpec((BLOCK, width), lambda i, c: (block_of(i, c), 0))
    half_spec = pl.BlockSpec((BLOCK, width // 2), lambda i, c: (block_of(i, c), 0))
    send_spec = pl.BlockSpec((BLOCK, width), lambda i, c: (jnp.minimum(i, steps - 1), 0))
    keep_spec = pl.BlockSpec((BLOCK, width), lambda i, c: (jnp.maximum(i - steps, 0), 0))
    ctx_specs = [
        pl.BlockSpec((a.shape[0], HEAD_DIM, BLOCK), lambda i, c: (0, 0, block_of(i, c)))
        for a in ctx
    ]
    dj_specs = [
        pl.BlockSpec((a.shape[0], BLOCK, 3 * HEAD_DIM), lambda i, c: (0, block_of(i, c), 0))
        for a in djs
    ]
    outs = [shape((held, width), BF16)] * 2 + [shape((held + EXTRA, width), BF16)] * 2
    return pl.pallas_call(
        close_kernel,
        grid_spec=pltpu.PrefetchScalarGridSpec(
            num_scalar_prefetch=1,
            grid=(rows // BLOCK,),
            in_specs=[row_spec] + [half_spec] * 4 + ctx_specs + dj_specs
            + [whole(a) for a in weights],
            out_specs=[send_spec, keep_spec, whole(outs[2]), whole(outs[3])],
            scratch_shapes=[pltpu.VMEM((EXTRA, width), F32)],
        ),
        out_shape=outs,
        compiler_params=pltpu.CompilerParams(
            dimension_semantics=("arbitrary",), vmem_limit_bytes=VMEM_BYTES
        ),
        cost_estimate=brief(),
        name="close_layer",
    )(core, x_seq, *hidden, *ctx, *djs, *weights)


def group_perm(n_row, n_col, target):
    pairs = []
    for r in range(n_row):
        for c in range(n_col):
            to = target(r, c // 2, c % 2)
            if to is not None:
                pairs.append((r * n_col + c, to[0] * n_col + 2 * to[1] + to[2]))
    return pairs


def swap_row(value):
    return lax.ppermute(value, "row", [(0, 1), (1, 0)])


def dp_inward(value):
    return lax.ppermute(value, "dp", [(0, 1), (3, 2)])


def dp_middle(value, inward):
    pair = (value.astype(F32) + inward.astype(F32)).astype(BF16)
    return pair, lax.ppermute(pair, "dp", [(1, 2), (2, 1)])


def dp_outward(pair, other):
    total = (pair.astype(F32) + other.astype(F32)).astype(BF16)
    return total, lax.ppermute(total, "dp", [(1, 0), (2, 3)])


def dp_finish(total, outward=None):
    if outward is None:
        return total
    place = lax.axis_index("dp")
    return jnp.where((place == 1) | (place == 2), total, outward).astype(F32)


def swap_sum(value, axis, size, bit):
    return value + lax.ppermute(value, axis, [(i, i ^ bit) for i in range(size)])


def local(
    block_input, w_qkv, b_qkv, w_in, b_in, w_dense, b_dense, w_out, b_out,
    ln_attn_gain, ln_attn_bias, ln_mlp_gain, ln_mlp_bias, segments, positions, d_out,
):
    n_row = lax.axis_size("row")
    n_col = lax.axis_size("col")
    n_dp = lax.axis_size("dp")
    row = lax.axis_index("row")
    col = lax.axis_index("col")
    half = block_input.shape[1]
    barrier = lax.optimization_barrier
    upper = col // 2
    core = col % 2
    home = row == upper
    heads = w_qkv.shape[1] // (3 * HEAD_DIM)

    spread = group_perm(
        n_row, n_col, lambda r, u, k: (r, 1 - u, k) if r == u else (1 - r, u, k)
    )
    cross = group_perm(n_row, n_col, lambda r, u, k: None if r == u else (1 - r, 1 - u, k))
    pair = group_perm(n_row, n_col, lambda r, u, k: (r, u, 1 - k))
    forward = group_perm(n_row, n_col, lambda r, u, k: (r, 1 - u, k) if r == u else None)
    collect = group_perm(
        n_row, n_col, lambda r, u, k: (1 - r, u, k) if r == u else (r, 1 - u, k)
    )

    chain = n_dp == 4
    inner = 3 * HEAD_DIM
    wq_t = w_qkv.T
    pack_a = jnp.concatenate([w_in[:, :half], w_out[:half]], axis=0)
    pack_b = jnp.concatenate([w_in[:, half:], w_out[half:], wq_t, w_dense], axis=0)
    norms = jnp.stack([ln_attn_gain, ln_attn_bias, ln_mlp_gain, ln_mlp_bias])
    core_at = core.reshape(1)

    at_seq = row * SEQ_LEN
    seg_seq = lax.dynamic_slice_in_dim(segments, at_seq, SEQ_LEN)
    pos_seq = lax.dynamic_slice_in_dim(positions, at_seq, SEQ_LEN)
    lane = jnp.arange(2 * HEAD_DIM) % HEAD_DIM
    freq_steps = (lane % (ROT // 2)).astype(F32) * (-2.0 * math.log(10000.0) / ROT)
    freq = jnp.where(lane < ROT, jnp.exp(freq_steps), 0.0)
    angles = pos_seq.astype(F32)[:, None] * freq[None, :]
    cos_table = jnp.cos(angles)
    sin_table = jnp.sin(angles)
    sin_up = jnp.where(lane < ROT // 2, -sin_table, 0.0)
    sin_down = jnp.where((lane >= ROT // 2) & (lane < ROT), sin_table, 0.0)

    def join(block, near, far):
        return jnp.concatenate(
            [jnp.where(home, block, near), jnp.where(home, near, far)], axis=1
        )

    d_out_f = d_out.astype(F32)
    norms_got = swap_row(norms)
    near_x = lax.ppermute(block_input, GROUP, spread)
    segc = seg_seq[:, None]
    go_in, cos_table, sin_up, sin_down, pack_a, pack_b, segc = barrier(
        (d_out, cos_table, sin_up, sin_down, pack_a, pack_b, segc)
    )
    near_go = lax.ppermute(go_in, GROUP, spread)
    near_x, norms, norms_got, pack_a = barrier((near_x, norms, norms_got, pack_a))
    far_x = lax.ppermute(near_x, GROUP, forward)
    got_a = swap_row(pack_a)
    far_go = lax.ppermute(near_go, GROUP, forward)
    x_mine = join(block_input, near_x, far_x)
    x_other = lax.ppermute(x_mine, GROUP, pair)
    far_go, got_a = barrier((far_go, got_a))
    go_mine = join(d_out, near_go, far_go)
    go_other = lax.ppermute(go_mine, GROUP, pair)
    got_b = swap_row(pack_b)
    norms = jnp.concatenate([norms, norms_got], axis=1)

    hid_a, dp_a, x_seq, go_seq, h_seq, own_a, send_a = mlp_first(
        core_at, x_mine, x_other, go_mine, go_other, w_in, w_out, got_a, b_in[None],
        norms[2:3], norms[3:4], norms[0:1], norms[1:2],
    )
    x_seq, send_a = barrier((x_seq, send_a))
    back_a = swap_row(send_a)
    hid_b, dp_b, own_b, send_b = mlp_second(
        x_seq, go_seq, w_in, w_out, got_b, b_in[None], norms[2:3], norms[3:4]
    )
    h_seq, send_b = barrier((h_seq, send_b))
    back_b = swap_row(send_b)
    width = wq_t.shape[0]
    heads_args = (
        wq_t, got_b, b_qkv.reshape(heads, 1, inner), w_dense, got_b,
        cos_table, sin_up, sin_down, segc, seg_seq[None, :],
    )

    def payload_sum(own, got):
        return (own.astype(F32) + got.astype(F32)).astype(BF16)

    heads01 = attn_head(0, heads - 1, h_seq, go_seq, *heads_args)
    go_seq, heads01, back_a, back_b = barrier((go_seq, heads01, back_a, back_b))
    back01 = swap_row(heads01[3])
    sum_a = payload_sum(own_a, back_a)
    sum_b = payload_sum(own_b, back_b)
    if chain:
        in_a = dp_inward(sum_a)
        in_b = dp_inward(sum_b)
    head2 = attn_head(heads - 1, 1, h_seq, go_seq, *heads_args)
    x_seq, head2, back01 = barrier((x_seq, head2, back01))
    back2 = swap_row(head2[3])
    sum_c = payload_sum(heads01[2], back01).reshape(-1, half)
    if chain:
        x_seq, in_a, sum_a = barrier((x_seq, in_a, sum_a))
        pair_a, other_a = dp_middle(sum_a, in_a)
        in_c = dp_inward(sum_c)
    done = [heads01, head2]
    mix_s, mix_k, dx_s, dx_k = close_layer(
        core_at, x_seq, [hid_a, hid_b, dp_a, dp_b], [a[0] for a in done], [a[1] for a in done],
        wq_t, w_dense, w_in, w_out, got_a, got_b, norms[0:1], norms[2:3],
    )
    if chain:
        mix_s, dx_s, in_b, sum_b, in_c, sum_c, pair_a, other_a = barrier(
            (mix_s, dx_s, in_b, sum_b, in_c, sum_c, pair_a, other_a)
        )
        totals_a = dp_outward(pair_a, other_a)
        pair_b, other_b = dp_middle(sum_b, in_b)
        pair_c, other_c = dp_middle(sum_c, in_c)
    mix_got = lax.ppermute(mix_s, GROUP, pair)
    dx_got = lax.ppermute(dx_s, GROUP, pair)
    mix_got, dx_got, back2 = barrier((mix_got, dx_got, back2))
    sum_d = payload_sum(head2[2], back2).reshape(-1, half)
    if chain:
        in_d = dp_inward(sum_d)

    def reduce_start(got, kept):
        low_sum = (kept.astype(F32) + got.astype(F32)).astype(BF16)
        near = lax.ppermute(
            jnp.where(home, low_sum[:, half:], low_sum[:, :half]), GROUP, collect
        )
        return near, lax.ppermute(low_sum[:, half:], GROUP, cross), low_sum[:, :half]

    def reduce_end(near, far, kept):
        return near.astype(F32) + jnp.where(home, kept, far).astype(F32)

    held = block_input.shape[0]
    norm_sums = dx_k[held : held + 4].astype(F32) + dx_got[held : held + 4].astype(F32)
    rest = norm_sums[:, :half] + swap_row(norm_sums[:, half:])
    rest = swap_sum(rest, "col", n_col, 2)
    mix_parts = reduce_start(mix_got, mix_k)
    dx_parts = reduce_start(dx_got[:held], dx_k[:held])
    if chain:
        rest = swap_sum(rest, "dp", 4, 1)
    if chain:
        in_d, sum_d, pair_b, other_b = barrier((in_d, sum_d, pair_b, other_b))
        totals_b = dp_outward(pair_b, other_b)
        pair_d, other_d = dp_middle(sum_d, in_d)
        mix_parts, dx_parts, pair_c, other_c, totals_a, rest = barrier(
            (mix_parts, dx_parts, pair_c, other_c, totals_a, rest)
        )
        rest = swap_sum(rest, "dp", 4, 2)
        totals_c = dp_outward(pair_c, other_c)
        totals_d = dp_outward(pair_d, other_d)
    dx_total = reduce_end(*dx_parts)
    if not chain:
        rest = lax.psum(rest, "dp")
        totals_a, totals_b, totals_c, totals_d = (
            (lax.psum(v.astype(F32), "dp"),) for v in (sum_a, sum_b, sum_c, sum_d)
        )

    def finish(totals, *at):
        return dp_finish(*[a[at] for a in totals])

    block_output = (
        block_input.astype(F32) + reduce_end(*mix_parts) + b_dense + b_out
    ).astype(BF16)
    d_input = d_out_f + dx_total
    upper_rows = slice(0, half)
    lower_rows = slice(half, 2 * half)
    grad_w_in = jnp.concatenate(
        [finish(totals_a, upper_rows), finish(totals_b, upper_rows)], axis=1
    )
    grad_w_out = jnp.concatenate(
        [finish(totals_a, lower_rows), finish(totals_b, lower_rows)], axis=0
    )
    deep = inner + HEAD_DIM
    step = deep + EXTRA
    split = [finish(totals_c, slice(n * step, n * step + step)) for n in range(heads - 1)]
    split = split + [finish(totals_d, slice(0, step))]
    grad_w_qkv = jnp.concatenate([a[:inner] for a in split], axis=0).T
    grad_w_dense = jnp.concatenate([a[inner:deep] for a in split], axis=0)
    grad_b_qkv = jnp.concatenate([a[deep, :inner] for a in split])
    grad_b_in = jnp.concatenate(
        [finish(totals_a, 2 * half), finish(totals_b, 2 * half)]
    )
    grad_b_out = finish(totals_a, 2 * half + 1)
    return (
        block_output, d_input, grad_w_qkv, grad_b_qkv, grad_w_in, grad_b_in,
        grad_w_dense, grad_b_out, grad_w_out, grad_b_out, rest[0], rest[1], rest[2], rest[3],
    )


def solution(mesh):
    token = P(("dp", "col"), "row")
    placed = (
        token, P("row", "col"), P("col"), P("row", "col"), P("col"), P("col", "row"), P("row"),
        P("col", "row"), P("row"), P("row"), P("row"), P("row"), P("row"), P("dp"), P("dp"), token,
    )
    return jax.shard_map(
        local,
        mesh=mesh,
        in_specs=placed,
        out_specs=(
            token, token, P("row", "col"), P("col"), P("row", "col"), P("col"), P("col", "row"),
            P("row"), P("col", "row"), P("row"), P("row"), P("row"), P("row"), P("row"),
        ),
        check_vma=False,
    )
```
